1024 devices in a mesh: expert: 64 (over y_lo, z, core), hidden: 16 (over x, y_hi).
Axes of the slice: x: 4, y: 8 (y_hi: 4, y_lo: 2; y = y_hi * 2 + y_lo), z: 16, core: 2. Of those that a mesh axis runs over, the one named last changes fastest.
Arguments:
- tokens: bfloat16 [1024, 2048], P('expert', 'hidden'), may hold values from -6 to 6
- out_cotangent: bfloat16 [1024, 2048], P('expert', 'hidden'), may hold values from -24 to 24
- expert_ids: int32 [1024, 8], P('expert'), may hold values from 0 to 63, all different within a row; in each aligned block of 16 rows (0 to 15, 16 to 31, ...) at most 4 rows name the same one
- gate_probs: float32 [1024, 8], P('expert'), may hold values from 0.05 to 0.35
- relocate: int32 [64], replicated, may hold values from 0 to 1, as said below
- w_gate: bfloat16 [64, 2048, 1536], P('expert', None, 'hidden'), may hold values from -0.125 to 0.125
- w_up: bfloat16 [64, 2048, 1536], P('expert', None, 'hidden'), may hold values from -0.125 to 0.125
- w_down: bfloat16 [64, 1536, 2048], P('expert', 'hidden'), may hold values from -0.15625 to 0.15625
- moment_gate: bfloat16 [64, 2048, 1536], P('expert', None, 'hidden'), may hold values from -3 to 3
- moment_up: bfloat16 [64, 2048, 1536], P('expert', None, 'hidden'), may hold values from -3 to 3
- moment_down: bfloat16 [64, 1536, 2048], P('expert', 'hidden'), may hold values from -3 to 3
Outputs:
- token_grad: bfloat16 [1024, 2048], P('expert', 'hidden')
- new_moment_gate: bfloat16 [64, 2048, 1536], P('expert', None, 'hidden')
- new_moment_up: bfloat16 [64, 2048, 1536], P('expert', None, 'hidden')
- new_moment_down: bfloat16 [64, 1536, 2048], P('expert', 'hidden')
The draws below stay inside these ranges and needn't reach their ends.
Inputs may be any that keep to these rules, and one draw needn't show every extreme that they name: `expert_ids`: in each group of 16 consecutive tokens no expert is named more than 4 times, a bound that some block reaches. relocate[s] equals relocate[(s + 32) mod 64]; exactly half of these pairs of slots have 1.
All inputs are finite; a program needn't handle non-finite values.
Results may differ from the reference program's by a relative error of at most 0.015.
Values may be sent and summed in bfloat16 or wider, within the bound.
A program may use at most 128 MiB of HBM per device.

```python
import math
import jax
import jax.numpy as jnp
import numpy as np
from jax import lax

D = 2048
FF = 1536
TOP = 8
TOK_GRP = 16
EXPERTS = 64
TOKENS = 1024
CAP = 4
N_EXPERT = 64
N_HIDDEN = 16


def draw_relocate(key, part):
    half = EXPERTS // 2
    order = jax.random.permutation(jax.random.fold_in(key, 17), half)
    pair_flag = (order < half // 2).astype(jnp.int32)
    return jnp.concatenate([pair_flag, pair_flag]).astype(jnp.int32)


def levels(own_key, dims, pieces, least, top_value):
    def one(dim, shards_of):
        heights = jax.random.uniform(jax.random.fold_in(jax.random.fold_in(own_key, 6), dim), (shards_of,), jnp.float32, least / len(pieces), top_value / len(pieces))
        return jnp.repeat(jnp.exp(heights), dims[dim] // shards_of).reshape((-1,) + (1,) * (len(dims) - dim - 1))

    loudness = one(*pieces[0])
    for cut in pieces[1:]:
        loudness = loudness * one(*cut)
    return loudness


def deal_out(own_key, own, number, rows, number_of, top, bound, slope):
    ranking = jax.random.permutation(own_key, number_of)
    crowded, common = shares(number_of, rows * top, bound, slope, True), shares(number_of, rows * top, bound, slope, False)
    places = jnp.arange(number_of)

    def named(lengths, rotation):
        used = int((lengths > 0).sum())
        fixed = max(1, used // 4)
        moved = fixed + (places - fixed + rotation * (used - fixed)) % max(1, number_of - fixed)
        return jnp.zeros((number_of,), jnp.int32).at[ranking[jnp.where(places < fixed, places, moved)]].set(jnp.asarray(lengths, jnp.int32))

    lengths = jnp.where(number % 4 == 0, named(crowded, number // 4), named(common, number - number // 4 - 1))
    mixed = jax.random.permutation(jax.random.fold_in(own, 3), number_of)
    source_of, taker = mixed[0:number_of // 2 * 2:2], mixed[1:number_of // 2 * 2:2]
    margin = jnp.minimum(lengths[source_of] - 1, bound - lengths[taker]) // 2
    margin = jnp.where((source_of == ranking[0]) | (taker == ranking[0]) | (lengths[taker] == 0), 0, jnp.maximum(margin, 0))
    moved = jax.random.randint(jax.random.fold_in(own, 4), (number_of // 2,), 0, 1 << 20) % (margin + 1)
    lengths = lengths.at[source_of].add(-moved).at[taker].add(moved)
    items = jnp.searchsorted(jnp.cumsum(lengths), jnp.arange(rows * top), side="right").astype(jnp.int32)
    grid = items.reshape(top, rows).T
    grid = grid[jax.random.permutation(jax.random.fold_in(own, 1), rows)]
    rotation = jax.random.randint(jax.random.fold_in(own, 2), (rows, 1), 0, top)
    return jnp.take_along_axis(grid, (jnp.arange(top)[None, :] + rotation) % top, axis=1)


def shares(number_of, total, bound, lean, full):
    portions = [(1 << 20) // math.isqrt(rank ** lean) + 1 for rank in range(1, number_of + 1)]
    largest = bound if full else min(bound, max(-(-total // number_of), total * portions[0] // sum(portions)))
    least = 1 if total - largest >= number_of - 1 else 0
    counts, rest = [largest] + [least] * (number_of - 1), total - largest - least * (number_of - 1)
    while rest > 0:
        movable = [i for i in range(1, number_of) if counts[i] < largest] or [i for i in range(1, number_of) if counts[i] < bound]
        mass, left = sum([portions[i] for i in movable]), rest
        for i in movable:
            extra = min(bound - counts[i], max(1, left * portions[i] // mass), rest)
            counts[i] = counts[i] + extra
            rest = rest - extra
    return np.array(counts)


def centred(own_key, shape, spread, most, cuts=(), held_as=jnp.bfloat16):
    factor_of = levels(own_key, shape, cuts, -0.22, 0.18) if cuts else 1.0
    array = jax.random.normal(own_key, shape, jnp.float32) * spread * factor_of
    return jnp.minimum(jnp.maximum(array, -most), most).astype(held_as)


def setup_inputs(seed: int = 0) -> dict:
    keys = jax.random.split(jax.random.key(seed), 12)
    tokens = centred(keys[0], (TOKENS, D), 1.0, 6.0, ((0, 64), (1, 16)))
    out_cotangent = centred(keys[1], (TOKENS, D), 4.0, 24.0, ((0, 64), (1, 16)))
    expert_ids_keys = jax.random.split(jax.random.fold_in(keys[2], 1), TOKENS // TOK_GRP)
    expert_ids_turns = jax.random.permutation(jax.random.fold_in(keys[2], 3), TOKENS // TOK_GRP)
    expert_ids = jax.vmap(lambda own, number: deal_out(jax.random.fold_in(keys[2], 2), own, number, TOK_GRP, EXPERTS, TOP, CAP, 2))(expert_ids_keys, expert_ids_turns).reshape((TOKENS, TOP))
    gate_probs = jnp.clip(0.05 + 0.29999999 * jax.random.uniform(keys[3], (TOKENS, TOP), jnp.float32) ** levels(keys[3], (TOKENS, TOP), ((0, 64),), -0.2, 0.2), 0.05, 0.35)
    relocate = draw_relocate(jax.random.fold_in(keys[11], 71), 0)
    w_gate = centred(keys[5], (EXPERTS, D, FF), D ** -0.5, 0.125, ((0, 64), (2, 16)))
    w_up = centred(keys[6], (EXPERTS, D, FF), D ** -0.5, 0.125, ((0, 64), (2, 16)))
    w_down = centred(keys[7], (EXPERTS, FF, D), FF ** -0.5, 0.15625, ((0, 64), (1, 16)))
    moment_gate = centred(keys[8], (EXPERTS, D, FF), 0.5, 3.0, ((0, 64), (2, 16)))
    moment_up = centred(keys[9], (EXPERTS, D, FF), 0.5, 3.0, ((0, 64), (2, 16)))
    moment_down = centred(keys[10], (EXPERTS, FF, D), 0.5, 3.0, ((0, 64), (1, 16)))
    return dict(tokens=tokens, out_cotangent=out_cotangent, expert_ids=expert_ids, gate_probs=gate_probs, relocate=relocate, w_gate=w_gate, w_up=w_up, w_down=w_down, moment_gate=moment_gate, moment_up=moment_up, moment_down=moment_down)


MOMENT_DECAY = 0.9


def reference(tokens, out_cotangent, expert_ids, gate_probs, relocate, w_gate, w_up, w_down, moment_gate, moment_up, moment_down):
    slots_per = N_EXPERT * CAP
    units = FF // N_HIDDEN
    flat_ids = expert_ids.reshape(N_EXPERT, TOK_GRP * TOP)
    experts_iota = jnp.arange(EXPERTS, dtype=jnp.int32)
    onehot = (flat_ids[:, :, None] == experts_iota[None, None, :]).astype(jnp.int32)
    ranks = jnp.sum((jnp.cumsum(onehot, axis=1) - onehot) * onehot, axis=2)
    group_iota = jnp.arange(N_EXPERT, dtype=jnp.int32)[:, None]
    positions = (flat_ids * slots_per + group_iota * CAP + ranks).reshape(TOKENS * TOP).astype(jnp.int32)
    token_index = (jnp.arange(TOKENS * TOP, dtype=jnp.int32) // TOP).astype(jnp.int32)
    table = jnp.zeros((EXPERTS * slots_per,), jnp.int32).at[positions].set(token_index + 1).reshape(EXPERTS, slots_per)
    prob_table = jnp.zeros((EXPERTS * slots_per,), jnp.float32).at[positions].set(gate_probs.reshape(TOKENS * TOP)).reshape(EXPERTS, slots_per)
    half = EXPERTS // 2
    owner = jnp.where(relocate == 1, (experts_iota + half) % EXPERTS, experts_iota).astype(jnp.int32)

    def one_slot(expert):
        rows = lax.dynamic_index_in_dim(table, expert, 0, keepdims=False)
        probs = lax.dynamic_index_in_dim(prob_table, expert, 0, keepdims=False)
        live = rows > 0
        picks = jnp.maximum(rows - 1, 0)
        x_rows = jnp.where(live[:, None], tokens[picks], jnp.zeros((), jnp.bfloat16)).astype(jnp.bfloat16)
        dy_rows = (probs[:, None] * out_cotangent[picks].astype(jnp.float32)).astype(jnp.bfloat16)
        gate_mat = w_gate[expert]
        up_mat = w_up[expert]
        down_mat = w_down[expert]
        gate_pre = jnp.dot(x_rows, gate_mat, preferred_element_type=jnp.float32)
        up_pre = jnp.dot(x_rows, up_mat, preferred_element_type=jnp.float32)
        back = jnp.dot(dy_rows, down_mat.T, preferred_element_type=jnp.float32)
        sig = jax.nn.sigmoid(gate_pre)
        act = gate_pre * sig
        hidden = (act * up_pre).astype(jnp.bfloat16)
        d_gate = (back * up_pre * sig * (1.0 + gate_pre * (1.0 - sig))).astype(jnp.bfloat16)
        d_up = (back * act).astype(jnp.bfloat16)
        grad_gate = jnp.dot(x_rows.T, d_gate, preferred_element_type=jnp.float32)
        grad_up = jnp.dot(x_rows.T, d_up, preferred_element_type=jnp.float32)
        grad_down = jnp.dot(hidden.T, dy_rows, preferred_element_type=jnp.float32)
        row_count = rows.shape[0]
        gate_blocks = d_gate.astype(jnp.float32).reshape(row_count, N_HIDDEN, units)
        up_blocks = d_up.astype(jnp.float32).reshape(row_count, N_HIDDEN, units)
        gate_w_blocks = gate_mat.astype(jnp.float32).reshape(D, N_HIDDEN, units)
        up_w_blocks = up_mat.astype(jnp.float32).reshape(D, N_HIDDEN, units)
        partial_value = jnp.einsum('rbf,dbf->brd', gate_blocks, gate_w_blocks, precision=lax.Precision.HIGHEST)
        partial_value = partial_value + jnp.einsum('rbf,dbf->brd', up_blocks, up_w_blocks, precision=lax.Precision.HIGHEST)
        rounded = lax.optimization_barrier(partial_value.astype(jnp.bfloat16))
        rows_grad = jnp.sum(rounded.astype(jnp.float32), axis=0)
        new_gate = (MOMENT_DECAY * moment_gate[expert].astype(jnp.float32) + (1.0 - MOMENT_DECAY) * grad_gate).astype(jnp.bfloat16)
        new_up = (MOMENT_DECAY * moment_up[expert].astype(jnp.float32) + (1.0 - MOMENT_DECAY) * grad_up).astype(jnp.bfloat16)
        new_down = (MOMENT_DECAY * moment_down[expert].astype(jnp.float32) + (1.0 - MOMENT_DECAY) * grad_down).astype(jnp.bfloat16)
        return new_gate, new_up, new_down, rows_grad

    new_gate, new_up, new_down, rows_grad = lax.map(one_slot, owner)
    slot_tables = table[owner]
    segment_ids = jnp.where(slot_tables > 0, slot_tables - 1, TOKENS).reshape(EXPERTS * slots_per).astype(jnp.int32)
    summed = jax.ops.segment_sum(rows_grad.reshape(EXPERTS * slots_per, D), segment_ids, num_segments=TOKENS + 1)
    token_grad = summed[:TOKENS].astype(jnp.bfloat16)
    return (token_grad, new_gate, new_up, new_down)
```

```python
import jax
import jax.numpy as jnp
from jax import lax
from jax.sharding import PartitionSpec as P

MOMENT_DECAY = 0.9
ROW_DIMS = (((0,), (0,)), ((), ()))
UNIT_DIMS = (((1,), (1,)), ((), ()))


def partner_2(block, axis, bit):
    count = lax.axis_size(axis)
    route = []
    for low in range(count):
        high = low | 1 << bit
        if high != low and high < count:
            route += [(low, high), (high, low)]
    return lax.ppermute(block, axis, route)


def routing_matrices(expert_ids, gate_probs, destination, capacity, expert_count):
    tok_rows, top_count = expert_ids.shape
    flat_ids = expert_ids.reshape(tok_rows * top_count)
    experts_iota = jnp.arange(expert_count, dtype=jnp.int32)
    onehot = (flat_ids[:, None] == experts_iota[None, :]).astype(jnp.int32)
    ranks = jnp.sum((jnp.cumsum(onehot, axis=0) - onehot) * onehot, axis=1)
    targets = jnp.sum(onehot * destination[None, :], axis=1)
    slots = (targets * capacity + ranks).reshape(tok_rows, top_count)
    slot_iota = jnp.arange(expert_count * capacity, dtype=jnp.int32)
    matches = slots[None, :, :] == slot_iota[:, None, None]
    placement = jnp.any(matches, axis=2).astype(jnp.float32)
    weighted = jnp.sum(jnp.where(matches, gate_probs[None, :, :], 0.0), axis=2)
    return (placement, weighted)


def update_moment(moment, gradient):
    return (MOMENT_DECAY * moment.astype(jnp.float32) + (1.0 - MOMENT_DECAY) * gradient).astype(
        jnp.bfloat16
    )


def on_device(
    tokens,
    out_cotangent,
    expert_ids,
    gate_probs,
    relocate,
    w_gate,
    w_up,
    w_down,
    moment_gate,
    moment_up,
    moment_down,
):
    expert_count = lax.axis_size("expert")
    tok_rows, top_count = expert_ids.shape
    capacity = min(tok_rows, 2 * tok_rows * top_count // expert_count)
    pair_bit = expert_count.bit_length() - 2
    experts_iota = jnp.arange(expert_count, dtype=jnp.int32)
    my_slot = lax.axis_index("expert")
    swapping = jnp.sum(jnp.where(experts_iota == my_slot, relocate, 0)) == 1
    gate_now, up_now, down_now = (w_gate[0], w_up[0], w_down[0])
    moments_now = (moment_gate[0], moment_up[0], moment_down[0])
    placement, weighted = routing_matrices(
        expert_ids, gate_probs, experts_iota, capacity, expert_count
    )
    rows_count = expert_count * capacity
    slice_width = tokens.shape[1]
    model_width = gate_now.shape[0]
    x_send = jnp.dot(
        placement.astype(jnp.bfloat16), tokens, preferred_element_type=jnp.float32
    ).astype(jnp.bfloat16)
    dy_send = jnp.dot(
        weighted, out_cotangent.astype(jnp.float32), precision=lax.Precision.HIGHEST
    ).astype(jnp.bfloat16)
    both = jnp.stack(
        [
            x_send.reshape(expert_count, capacity, slice_width),
            dy_send.reshape(expert_count, capacity, slice_width),
        ],
        axis=1,
    )
    both = lax.all_to_all(both, "expert", split_axis=0, concat_axis=0, tiled=True)
    both = jnp.swapaxes(both, 0, 1).reshape(2 * rows_count, slice_width)
    both = lax.all_gather(both, "hidden", axis=1, tiled=True)
    x_full, dy_full = both[:rows_count], both[rows_count:]
    gate_pre = jnp.dot(x_full, gate_now, preferred_element_type=jnp.float32)
    up_pre = jnp.dot(x_full, up_now, preferred_element_type=jnp.float32)
    back = lax.dot_general(dy_full, down_now, UNIT_DIMS, preferred_element_type=jnp.float32)
    sig = jax.nn.sigmoid(gate_pre)
    act = gate_pre * sig
    hidden = (act * up_pre).astype(jnp.bfloat16)
    d_gate = (back * up_pre * sig * (1.0 + gate_pre * (1.0 - sig))).astype(jnp.bfloat16)
    d_up = (back * act).astype(jnp.bfloat16)
    grad_gate = lax.dot_general(x_full, d_gate, ROW_DIMS, preferred_element_type=jnp.float32)
    grad_up = lax.dot_general(x_full, d_up, ROW_DIMS, preferred_element_type=jnp.float32)
    grad_down = lax.dot_general(hidden, dy_full, ROW_DIMS, preferred_element_type=jnp.float32)
    partial_value = lax.dot_general(gate_now, d_gate, UNIT_DIMS, preferred_element_type=jnp.float32)
    partial_value = partial_value + lax.dot_general(
        up_now, d_up, UNIT_DIMS, preferred_element_type=jnp.float32
    )
    fresh_gate = update_moment(moments_now[0], grad_gate)
    fresh_up = update_moment(moments_now[1], grad_up)
    fresh_down = update_moment(moments_now[2], grad_down)
    arrived = partner_2((fresh_gate, fresh_up, fresh_down), "expert", pair_bit)
    fresh_gate, fresh_up, fresh_down = [
        jnp.where(swapping, incoming, kept)
        for incoming, kept in zip(arrived, (fresh_gate, fresh_up, fresh_down))
    ]
    summed = lax.psum_scatter(
        partial_value.astype(jnp.bfloat16), "hidden", scatter_dimension=0, tiled=True
    ).astype(jnp.float32)
    summed = summed.T.reshape(expert_count, capacity, slice_width)
    returned = lax.all_to_all(
        summed.astype(jnp.bfloat16), "expert", split_axis=0, concat_axis=0, tiled=True
    ).astype(summed.dtype)
    token_sum = jnp.dot(
        placement.T,
        returned.reshape(rows_count, slice_width),
        precision=lax.Precision.HIGHEST,
        preferred_element_type=jnp.float32,
    )
    token_grad = token_sum.astype(jnp.bfloat16)
    return (token_grad, fresh_gate[None], fresh_up[None], fresh_down[None])


def solution(mesh):
    return jax.shard_map(
        on_device,
        mesh=mesh,
        in_specs=(
            P("expert", "hidden"),
            P("expert", "hidden"),
            P("expert", None),
            P("expert", None),
            P(),
            P("expert", None, "hidden"),
            P("expert", None, "hidden"),
            P("expert", "hidden", None),
            P("expert", None, "hidden"),
            P("expert", None, "hidden"),
            P("expert", "hidden", None),
        ),
        out_specs=(
            P("expert", "hidden"),
            P("expert", None, "hidden"),
            P("expert", None, "hidden"),
            P("expert", "hidden", None),
        ),
        check_vma=False,
    )
```

```python
import functools

import jax
import jax.numpy as jnp
from jax import lax
from jax.experimental import pallas as pl
from jax.experimental.pallas import tpu as pltpu
from jax.sharding import PartitionSpec as P

MOMENT_DECAY = 0.9
CAPACITY = 4
LANES = 128
SIDE = 4
MESH = pl.DeviceIdType.MESH
NT = (((1,), (1,)), ((), ()))
NN = (((1,), (0,)), ((), ()))


def routing(expert_ids, gate_probs, expert_count):
    tok_rows, top_count = expert_ids.shape
    flat_ids = expert_ids.reshape(tok_rows * top_count)
    experts_iota = jnp.arange(expert_count, dtype=jnp.int32)
    onehot = (flat_ids[:, None] == experts_iota[None, :]).astype(jnp.int32)
    ranks = jnp.sum((jnp.cumsum(onehot, axis=0) - onehot) * onehot, axis=1)
    slots = (flat_ids * (2 * CAPACITY) + ranks).reshape(tok_rows, top_count)
    slot_iota = jnp.arange(expert_count * 2 * CAPACITY, dtype=jnp.int32)
    take_x = slots[None, :, :] == slot_iota[:, None, None]
    take_dy = slots[None, :, :] + CAPACITY == slot_iota[:, None, None]
    placement = jnp.any(take_x, axis=2).astype(jnp.bfloat16)
    weighted = jnp.sum(jnp.where(take_dy, gate_probs[None, :, :], 0.0), axis=2)
    back_slots = slots[:, :, None] == slot_iota[None, None, :]
    collect = jnp.any(back_slots, axis=1).astype(jnp.bfloat16)
    return placement, weighted, collect


def dot(a, b, dims):
    return lax.dot_general(a, b, dims, preferred_element_type=jnp.float32)


def kernel(
    send_ref,
    collect_ref,
    wg_ref,
    wu_ref,
    wd_ref,
    mg_ref,
    mu_ref,
    md_ref,
    tok_ref,
    own_ref,
    got_ref,
    w,
    m,
    g,
    acc,
    sides,
    p,
    buf_a,
    buf_b,
    buf_c,
    buf_d,
    tmp_r,
    tmp_l,
    q,
    y_a,
    y_b,
    y_c,
    y_d,
    y_r,
    y_l,
    back,
    ret,
    load_sem,
    a2a_sem,
    gs_sem,
    gr_sem,
    ps_sem,
    pr_sem,
    ms_sem,
    mr_sem,
    ret_sem,
):
    count = send_ref.shape[0]
    units = wg_ref.shape[0]
    wide = count * 2 * CAPACITY
    rows = count * CAPACITY
    half = count // 2
    e = lax.axis_index("expert")
    hid = lax.axis_index("hidden")
    x, y = lax.div(hid, SIDE), lax.rem(hid, SIDE)

    def h_at(dx, dy):
        return lax.rem(x + dx, SIDE) * SIDE + lax.rem(y + dy, SIDE)

    def peer(de, dx, dy):
        return (lax.rem(e + de, count), h_at(dx, dy))

    x_right, x_left = peer(0, 1, 0), peer(0, 3, 0)
    y_right, y_left = peer(0, 0, 1), peer(0, 0, 3)
    partner = peer(half, 0, 0)

    loads = [
        pltpu.make_async_copy(src, dst.at[pl.ds(i * units, units)], load_sem.at[j * 3 + i])
        for j, (dst, group) in enumerate(
            ((w, (wg_ref, wu_ref, wd_ref)), (m, (mg_ref, mu_ref, md_ref)))
        )
        for i, src in enumerate(group)
    ]
    for load in loads:
        load.start()

    barrier = pltpu.get_barrier_semaphore()

    def greet(i, carry):
        pl.semaphore_signal(barrier, inc=1, device_id=peer(i, 0, 0), device_id_type=MESH)
        return carry

    lax.fori_loop(1, count, greet, 0)
    for near in (x_right, x_left, y_right, y_left):
        pl.semaphore_signal(barrier, inc=1, device_id=near, device_id_type=MESH)
    pl.semaphore_wait(barrier, count - 1 + 4)

    def remote(src, dst, ssem, rsem, to):
        return pltpu.make_async_remote_copy(
            src_ref=src,
            dst_ref=dst,
            send_sem=ssem,
            recv_sem=rsem,
            device_id=to,
            device_id_type=MESH,
        )

    me = h_at(0, 0)

    def deal(i, carry):
        to = peer(i, 0, 0)
        remote(send_ref.at[to[0]], g.at[me, e], a2a_sem.at[0], a2a_sem.at[1], to).start()
        return carry

    lax.fori_loop(1, count, deal, 0)
    keep = pltpu.make_async_copy(send_ref.at[e], g.at[me, e], a2a_sem.at[2])
    keep.start()
    keep.wait()
    dealt = remote(
        send_ref.at[pl.ds(0, count - 1)],
        g.at[me, pl.ds(0, count - 1)],
        a2a_sem.at[0],
        a2a_sem.at[1],
        x_right,
    )
    dealt.wait_recv()

    sent = []

    def push(src, dst, sems, n, to):
        copy = remote(src, dst, sems[0].at[n], sems[1].at[n], to)
        copy.start()
        sent.append(copy)
        return copy

    gs = (gs_sem, gr_sem)

    def x_out(n, dy):
        h = h_at(0, dy)
        return (
            push(g.at[h], g.at[h], gs, 4 + 4 * n, x_right),
            push(g.at[h], g.at[h], gs, 5 + 4 * n, x_left),
        )

    def x_forward(n, dy, from_left, from_right):
        from_left.wait_recv()
        h = h_at(3, dy)
        low = g.at[h, pl.ds(0, half)]
        a = push(low, low, gs, 6 + 4 * n, x_right)
        from_right.wait_recv()
        h = h_at(1, dy)
        high = g.at[h, pl.ds(half, half)]
        b = push(high, high, gs, 7 + 4 * n, x_left)
        return a, b

    def absorb(dx, dy, first=False):
        h = h_at(dx, dy)
        cols = pl.ds(pl.multiple_of(h * LANES, LANES), LANES)
        term = dot(w[:, cols], g[h].reshape(wide, LANES), NT)
        if first:
            acc[...] = term
        else:
            acc[...] += term

    from_yl = push(g.at[me], g.at[me], gs, 0, y_right)
    from_yr = push(g.at[me], g.at[me], gs, 1, y_left)
    in0 = x_out(0, 0)
    for load in loads[:3]:
        load.wait()
    absorb(0, 0, True)
    from_yl.wait_recv()
    h = h_at(0, 3)
    low = g.at[h, pl.ds(0, half)]
    opp_low = push(low, low, gs, 2, y_right)
    in1 = x_out(1, 3)
    from_yr.wait_recv()
    h = h_at(0, 1)
    high = g.at[h, pl.ds(half, half)]
    opp_high = push(high, high, gs, 3, y_left)
    in2 = x_out(2, 1)
    fwd0 = x_forward(0, 0, *in0)
    absorb(0, 3)
    absorb(0, 1)
    opp_low.wait_recv()
    opp_high.wait_recv()
    in3 = x_out(3, 2)
    absorb(0, 2)
    absorb(3, 0)
    absorb(1, 0)
    fwd1 = x_forward(1, 3, *in1)
    absorb(3, 3)
    absorb(1, 3)
    fwd2 = x_forward(2, 1, *in2)
    absorb(3, 1)
    absorb(1, 1)
    fwd3 = x_forward(3, 2, *in3)
    absorb(3, 2)
    absorb(1, 2)
    for dy, arrivals in ((0, fwd0), (3, fwd1), (1, fwd2), (2, fwd3)):
        for copy in arrivals:
            copy.wait_recv()
        absorb(2, dy)

    gate = acc[pl.ds(0, units), :]
    up = acc[pl.ds(units, units), :]
    down = pltpu.roll(acc[pl.ds(2 * units, units), :], wide - CAPACITY, 1)
    lane = lax.broadcasted_iota(jnp.int32, (units, wide), 1)
    is_x = jnp.bitwise_and(lane, 2 * CAPACITY - 1) < CAPACITY
    sig = jax.nn.sigmoid(gate)
    act = gate * sig
    d_gate = down * up * sig * (1.0 + gate * (1.0 - sig))
    d_up = down * act
    hidden = pltpu.roll(jnp.where(is_x, act * up, 0.0), CAPACITY, 1)
    sides[pl.ds(0, units), :] = jnp.where(is_x, d_gate, 0.0).astype(jnp.bfloat16)
    sides[pl.ds(units, units), :] = jnp.where(is_x, d_up, 0.0).astype(jnp.bfloat16)
    sides[pl.ds(2 * units, units), :] = hidden.astype(jnp.bfloat16)

    row = lax.broadcasted_iota(jnp.int32, (rows, wide), 0)
    col = lax.broadcasted_iota(jnp.int32, (rows, wide), 1)
    slot = (row // CAPACITY) * (2 * CAPACITY) + jnp.bitwise_and(row, CAPACITY - 1)
    compact = (slot == col).astype(jnp.float32).astype(jnp.bfloat16)
    d_rows = dot(compact, sides[pl.ds(0, 2 * units), :], NT).astype(jnp.bfloat16)

    def quarter(dx):
        block = lax.rem(x + dx, SIDE)
        cols = pl.ds(pl.multiple_of(block * (SIDE * LANES), LANES), SIDE * LANES)
        value = dot(d_rows, w[pl.ds(0, 2 * units), cols], NN).astype(jnp.bfloat16)
        for j in range(SIDE):
            p[block * SIDE + j] = value[:, j * LANES : (j + 1) * LANES]
        return block * SIDE

    ps = (ps_sem, pr_sem)
    o = quarter(2)
    from_a = push(p.at[pl.ds(o, 2)], buf_a, ps, 0, x_right)
    from_b = push(p.at[pl.ds(o + 2, 2)], buf_b, ps, 1, x_left)
    r = quarter(1)
    c_high = push(p.at[pl.ds(r + 2, 2)], buf_c.at[pl.ds(2, 2)], ps, 2, x_right)
    l = quarter(3)
    d_low = push(p.at[pl.ds(l, 2)], buf_d.at[pl.ds(0, 2)], ps, 3, x_left)
    s = quarter(0)

    for load in loads[3:]:
        load.wait()

    def fresh(i):
        span = pl.ds(i * units, units)
        for k in range(SIDE * SIDE // 2):
            rhs = jnp.concatenate(
                [g[2 * k].reshape(wide, LANES), g[2 * k + 1].reshape(wide, LANES)], axis=1
            )
            grad = dot(sides[span, :], rhs, NN)
            cols = pl.ds(2 * k * LANES, 2 * LANES)
            old = m[span, cols].astype(jnp.float32)
            own_ref[span, cols] = (MOMENT_DECAY * old + (1.0 - MOMENT_DECAY) * grad).astype(
                jnp.bfloat16
            )
        return push(own_ref.at[span], got_ref.at[span], (ms_sem, mr_sem), i, partner)

    swaps = [fresh(0)]

    def add(a, b):
        return (a.astype(jnp.float32) + b.astype(jnp.float32)).astype(jnp.bfloat16)

    from_a.wait_recv()
    tmp_r[...] = add(p[pl.ds(r, 2)], buf_a[...])
    c_low = push(tmp_r, buf_c.at[pl.ds(0, 2)], ps, 4, x_right)
    from_b.wait_recv()
    tmp_l[...] = add(p[pl.ds(l + 2, 2)], buf_b[...])
    d_high = push(tmp_l, buf_d.at[pl.ds(2, 2)], ps, 5, x_left)
    for copy in (c_high, d_low, c_low, d_high):
        copy.wait_recv()
    f32 = jnp.float32
    q[...] = (
        p[pl.ds(s, SIDE)].astype(f32) + buf_c[...].astype(f32) + buf_d[...].astype(f32)
    ).astype(jnp.bfloat16)

    top, low_rows = pl.ds(0, rows // 2), pl.ds(rows // 2, rows // 2)
    yo, yr, yl = lax.rem(y + 2, SIDE), lax.rem(y + 1, SIDE), lax.rem(y + 3, SIDE)
    from_a = push(q.at[yo, top], y_a, ps, 6, y_right)
    from_b = push(q.at[yo, low_rows], y_b, ps, 7, y_left)
    c_high = push(q.at[yr, low_rows], y_c.at[low_rows], ps, 8, y_right)
    d_low = push(q.at[yl, top], y_d.at[top], ps, 9, y_left)
    from_a.wait_recv()
    y_r[...] = add(q[yr, top], y_a[...])
    c_low = push(y_r, y_c.at[top], ps, 10, y_right)
    from_b.wait_recv()
    y_l[...] = add(q[yl, low_rows], y_b[...])
    d_high = push(y_l, y_d.at[low_rows], ps, 11, y_left)
    swaps.append(fresh(1))
    for copy in (c_high, d_low, c_low, d_high):
        copy.wait_recv()
    total = (q[y].astype(f32) + y_c[...].astype(f32) + y_d[...].astype(f32)).astype(jnp.bfloat16)

    row = lax.broadcasted_iota(jnp.int32, (wide, rows), 0)
    col = lax.broadcasted_iota(jnp.int32, (wide, rows), 1)
    slot = (col // CAPACITY) * (2 * CAPACITY) + jnp.bitwise_and(col, CAPACITY - 1)
    spread = (slot == row).astype(jnp.float32).astype(jnp.bfloat16)
    back[...] = dot(spread, total, NN).astype(jnp.bfloat16).reshape(back.shape)

    def give(i, carry):
        to = peer(i, 0, 0)
        remote(back.at[to[0]], ret.at[e], ret_sem.at[0], ret_sem.at[1], to).start()
        return carry

    lax.fori_loop(1, count, give, 0)
    swaps.append(fresh(2))
    keep = pltpu.make_async_copy(back.at[e], ret.at[e], ret_sem.at[2])
    keep.start()
    keep.wait()
    given = remote(
        back.at[pl.ds(0, count - 1)],
        ret.at[pl.ds(0, count - 1)],
        ret_sem.at[0],
        ret_sem.at[1],
        x_right,
    )
    given.wait_recv()
    tok_ref[...] = dot(collect_ref[...], ret[...].reshape(wide, LANES), NN).astype(jnp.bfloat16)

    for copy in swaps:
        copy.wait_recv()
    for copy in sent:
        copy.wait_send()
    dealt.wait_send()
    given.wait_send()


def run_kernel(send, collect, weights, moments):
    count = send.shape[0]
    units, width = weights[0].shape
    wide, rows = count * 2 * CAPACITY, count * CAPACITY
    blocks = SIDE * SIDE
    bf16, f32 = jnp.bfloat16, jnp.float32
    vmem, dma = pltpu.VMEM, pltpu.SemaphoreType.DMA
    return pl.pallas_call(
        kernel,
        out_shape=(
            jax.ShapeDtypeStruct((collect.shape[0], LANES), bf16),
            jax.ShapeDtypeStruct((3 * units, width), bf16),
            jax.ShapeDtypeStruct((3 * units, width), bf16),
        ),
        in_specs=[pl.BlockSpec(memory_space=vmem)] * 2 + [pl.BlockSpec(memory_space=pl.ANY)] * 6,
        out_specs=(
            pl.BlockSpec(memory_space=vmem),
            pl.BlockSpec(memory_space=vmem),
            pl.BlockSpec(memory_space=pl.ANY),
        ),
        scratch_shapes=[
            vmem((3 * units, width), bf16),
            vmem((3 * units, width), bf16),
            vmem((blocks, count, 2 * CAPACITY, LANES), bf16),
            vmem((3 * units, wide), f32),
            vmem((3 * units, wide), bf16),
            vmem((blocks, rows, LANES), bf16),
            vmem((2, rows, LANES), bf16),
            vmem((2, rows, LANES), bf16),
            vmem((4, rows, LANES), bf16),
            vmem((4, rows, LANES), bf16),
            vmem((2, rows, LANES), bf16),
            vmem((2, rows, LANES), bf16),
            vmem((4, rows, LANES), bf16),
            vmem((rows // 2, LANES), bf16),
            vmem((rows // 2, LANES), bf16),
            vmem((rows, LANES), bf16),
            vmem((rows, LANES), bf16),
            vmem((rows // 2, LANES), bf16),
            vmem((rows // 2, LANES), bf16),
            vmem((count, 2 * CAPACITY, LANES), bf16),
            vmem((count, 2 * CAPACITY, LANES), bf16),
            dma((6,)),
            dma((3,)),
            dma((20,)),
            dma((20,)),
            dma((12,)),
            dma((12,)),
            dma((3,)),
            dma((3,)),
            dma((3,)),
        ],
        compiler_params=pltpu.CompilerParams(
            collective_id=0, has_side_effects=True, vmem_limit_bytes=48 * 1024 * 1024
        ),
        name="experts",
    )(send, collect, *weights, *moments)


def on_device(
    tokens,
    out_cotangent,
    expert_ids,
    gate_probs,
    relocate,
    w_gate,
    w_up,
    w_down,
    moment_gate,
    moment_up,
    moment_down,
):
    count = lax.axis_size("expert")
    my_slot = lax.axis_index("expert")
    experts_iota = jnp.arange(count, dtype=jnp.int32)
    swapping = jnp.sum(jnp.where(experts_iota == my_slot, relocate, 0)) == 1
    placement, weighted, collect = routing(expert_ids, gate_probs, count)
    x_part = jnp.dot(placement, tokens, preferred_element_type=jnp.float32)
    dy_part = jnp.dot(
        weighted, out_cotangent.astype(jnp.float32), precision=lax.Precision.HIGHEST
    )
    send = (x_part + dy_part).astype(jnp.bfloat16).reshape(count, 2 * CAPACITY, LANES)
    token_grad, own, got = run_kernel(
        send,
        collect,
        (w_gate[0].T, w_up[0].T, w_down[0]),
        (moment_gate[0].T, moment_up[0].T, moment_down[0]),
    )
    units = w_down.shape[1]
    fresh = [
        jnp.where(swapping, got[i * units : (i + 1) * units], own[i * units : (i + 1) * units])
        for i in range(3)
    ]
    return (token_grad, fresh[0].T[None], fresh[1].T[None], fresh[2][None])


def solution(mesh):
    return jax.shard_map(
        on_device,
        mesh=mesh,
        in_specs=(
            P("expert", "hidden"),
            P("expert", "hidden"),
            P("expert", None),
            P("expert", None),
            P(),
            P("expert", None, "hidden"),
            P("expert", None, "hidden"),
            P("expert", "hidden", None),
            P("expert", None, "hidden"),
            P("expert", None, "hidden"),
            P("expert", "hidden", None),
        ),
        out_specs=(
            P("expert", "hidden"),
            P("expert", None, "hidden"),
            P("expert", None, "hidden"),
            P("expert", "hidden", None),
        ),
        check_vma=False,
    )
```

```python
import functools

import jax
import jax.numpy as jnp
from jax import lax
from jax.experimental import pallas as pl
from jax.experimental.pallas import tpu as pltpu
from jax.sharding import PartitionSpec as P

MOMENT_DECAY = 0.9
CAPACITY = 4
LANES = 128
SIDE = 4
MESH = pl.DeviceIdType.MESH
NT = (((1,), (1,)), ((), ()))
NN = (((1,), (0,)), ((), ()))
TN = (((0,), (0,)), ((), ()))


def dot(a, b, dims):
    return lax.dot_general(a, b, dims, preferred_element_type=jnp.float32)


def kernel(
    ids_ref,
    probs_ref,
    tokens_ref,
    cot_ref,
    relocate_ref,
    wg_ref,
    wu_ref,
    wd_ref,
    mg_ref,
    mu_ref,
    md_ref,
    tok_ref,
    flag_ref,
    own_ref,
    got_ref,
    ids,
    probs,
    toks,
    cots,
    moved,
    send,
    collect,
    own,
    w,
    m,
    g,
    acc,
    sides,
    p,
    buf_a,
    buf_b,
    buf_c,
    buf_d,
    tmp_r,
    tmp_l,
    q,
    y_a,
    y_b,
    y_c,
    y_d,
    y_r,
    y_l,
    back,
    ret,
    load_sem,
    a2a_sem,
    gs_sem,
    gr_sem,
    ps_sem,
    pr_sem,
    ms_sem,
    mr_sem,
    ret_sem,
    own_sem,
):
    count = send.shape[0]
    units = wg_ref.shape[0]
    tok_rows = tokens_ref.shape[0]
    wide = count * 2 * CAPACITY
    rows = count * CAPACITY
    half = count // 2
    e = lax.axis_index("expert")
    hid = lax.axis_index("hidden")
    x, y = lax.div(hid, SIDE), lax.rem(hid, SIDE)

    def h_at(dx, dy):
        return lax.rem(x + dx, SIDE) * SIDE + lax.rem(y + dy, SIDE)

    def peer(de, dx, dy):
        return (lax.rem(e + de, count), h_at(dx, dy))

    x_right, x_left = peer(0, 1, 0), peer(0, 3, 0)
    y_right, y_left = peer(0, 0, 1), peer(0, 0, 3)
    partner = peer(half, 0, 0)

    small = [
        pltpu.make_async_copy(src, dst, load_sem.at[6 + i])
        for i, (src, dst) in enumerate(
            (
                (ids_ref, ids),
                (probs_ref, probs),
                (tokens_ref, toks),
                (cot_ref, cots),
                (relocate_ref, moved),
            )
        )
    ]
    for load in small:
        load.start()
    loads = [
        pltpu.make_async_copy(src, dst.at[pl.ds(i * units, units)], load_sem.at[j * 3 + i])
        for j, (dst, group) in enumerate(
            ((w, (wg_ref, wu_ref, wd_ref)), (m, (mg_ref, mu_ref, md_ref)))
        )
        for i, src in enumerate(group)
    ]
    for load in loads:
        load.start()

    barrier = pltpu.get_barrier_semaphore()

    def greet(i, carry):
        pl.semaphore_signal(barrier, inc=1, device_id=peer(i, 0, 0), device_id_type=MESH)
        return carry

    lax.fori_loop(1, count, greet, 0)
    for near in (x_right, x_left, y_right, y_left):
        pl.semaphore_signal(barrier, inc=1, device_id=near, device_id_type=MESH)

    for load in small:
        load.wait()
    f32, bf16 = jnp.float32, jnp.bfloat16
    slot = lax.broadcasted_iota(jnp.int32, (wide, tok_rows), 0)
    expert = slot // (2 * CAPACITY)
    place = jnp.bitwise_and(slot, 2 * CAPACITY - 1)
    named = jnp.zeros((wide, tok_rows), f32)
    scale = jnp.zeros((wide, tok_rows), f32)
    for k in range(ids_ref.shape[0]):
        hit = expert == ids[k : k + 1, :]
        named += jnp.where(hit, 1.0, 0.0)
        scale += jnp.where(hit, probs[k : k + 1, :], 0.0)
    earlier = lax.broadcasted_iota(jnp.int32, (tok_rows, tok_rows), 0)
    later = lax.broadcasted_iota(jnp.int32, (tok_rows, tok_rows), 1)
    before = jnp.where(earlier < later, 1.0, 0.0).astype(bf16)
    rank = dot(named.astype(bf16), before, NN)
    want = jnp.bitwise_and(place, CAPACITY - 1).astype(f32)
    chosen = jnp.where(rank == want, named, 0.0)
    take_x = jnp.where(place < CAPACITY, chosen, 0.0).astype(bf16)
    scale = jnp.where(place < CAPACITY, 0.0, chosen * scale)
    collect[...] = take_x
    dealing = dot(take_x, toks[...], NN)
    for _ in range(3):
        part = scale.astype(bf16)
        dealing += dot(part, cots[...], NN)
        scale = scale - part.astype(f32)
    send[...] = dealing.astype(bf16).reshape(send.shape)
    lanes = lax.broadcasted_iota(jnp.int32, moved.shape, 1)
    flag = jnp.sum(jnp.where(lanes == e, moved[...], 0), axis=1, keepdims=True)
    flag_ref[...] = jnp.broadcast_to(flag.astype(f32), flag_ref.shape)
    pl.semaphore_wait(barrier, count - 1 + 4)

    def remote(src, dst, ssem, rsem, to):
        return pltpu.make_async_remote_copy(
            src_ref=src,
            dst_ref=dst,
            send_sem=ssem,
            recv_sem=rsem,
            device_id=to,
            device_id_type=MESH,
        )

    me = h_at(0, 0)

    def deal(n):
        def step(i, carry):
            to = peer(i, 0, 0)
            remote(send.at[to[0]], g.at[me, i], a2a_sem.at[0], a2a_sem.at[n], to).start()
            return carry

        return step

    lax.fori_loop(1, half, deal(1), 0)
    lax.fori_loop(half, count, deal(2), 0)
    keep = pltpu.make_async_copy(send.at[e], g.at[me, 0], a2a_sem.at[3])
    keep.start()

    def dealt(first, size, n):
        span = pl.ds(first, size)
        return remote(send.at[span], g.at[me, span], a2a_sem.at[0], a2a_sem.at[n], x_right)

    sent = []

    def push(src, dst, sems, n, to):
        copy = remote(src, dst, sems[0].at[n], sems[1].at[n], to)
        copy.start()
        sent.append(copy)
        return copy

    gs = (gs_sem, gr_sem)

    fold = half // 2

    def part(h, c):
        return g.at[h, pl.ds(c * half, half)]

    def low(h, c):
        return g.at[h, pl.ds(c * half, fold)]

    def high(h, c):
        return g.at[h, pl.ds(c * half + fold, fold)]

    def both(pick, h, c, n, right, left):
        src = pick(h, c)
        return push(src, src, gs, 20 * c + n, right), push(src, src, gs, 20 * c + n + 1, left)

    def x_out(n, dy, c):
        return both(part, h_at(0, dy), c, 4 + 4 * n, x_right, x_left)

    def forward(n, c, left_h, right_h, arrivals, right, left):
        arrivals[0].wait_recv()
        a = low(left_h, c)
        a = push(a, a, gs, 20 * c + n, right)
        arrivals[1].wait_recv()
        b = high(right_h, c)
        return a, push(b, b, gs, 20 * c + n + 1, left)

    def x_forward(n, dy, c, arrivals):
        return forward(6 + 4 * n, c, h_at(3, dy), h_at(1, dy), arrivals, x_right, x_left)

    def absorb(dx, dy, c, first=False):
        h = h_at(dx, dy)
        cols = pl.ds(pl.multiple_of(h * LANES, LANES), LANES)
        mine = pl.ds(c * (wide // 2), wide // 2)
        term = dot(w[:, cols], part(h, c)[...].reshape(wide // 2, LANES), NT)
        if first:
            acc[:, mine] = term
        else:
            acc[:, mine] += term

    streams = (0, 1)
    y_in, x_in, x_fwd, opp = {}, {}, {}, {}

    def begin(c):
        y_in[c] = both(part, me, c, 0, y_right, y_left)
        x_in[c, 0] = x_out(0, 0, c)

    keep.wait()
    dealt(1, half - 1, 1).wait_recv()
    begin(0)
    for load in loads[:3]:
        load.wait()
    absorb(0, 0, 0, True)
    dealt(half, half, 2).wait_recv()
    begin(1)
    absorb(0, 0, 1, True)
    for c in streams:
        opp[c] = forward(2, c, h_at(0, 3), h_at(0, 1), y_in[c], y_right, y_left)
        x_in[c, 3] = x_out(1, 3, c)
        x_in[c, 1] = x_out(2, 1, c)
        x_fwd[c, 0] = x_forward(0, 0, c, x_in[c, 0])
        absorb(0, 3, c)
        absorb(0, 1, c)
    for c in streams:
        for copy in opp[c]:
            copy.wait_recv()
        x_in[c, 2] = x_out(3, 2, c)
        absorb(3, 0, c)
        absorb(1, 0, c)
        x_fwd[c, 3] = x_forward(1, 3, c, x_in[c, 3])
        absorb(3, 3, c)
        absorb(1, 3, c)
        x_fwd[c, 1] = x_forward(2, 1, c, x_in[c, 1])
        absorb(0, 2, c)
        absorb(3, 1, c)
        absorb(1, 1, c)

    def finish(c, dy):
        for copy in x_fwd[c, dy]:
            copy.wait_recv()
        absorb(2, dy, c)

    for c in streams:
        finish(c, 0)
        finish(c, 3)
        x_fwd[c, 2] = x_forward(3, 2, c, x_in[c, 2])
        absorb(3, 2, c)
        absorb(1, 2, c)
    for c in streams:
        finish(c, 1)
        finish(c, 2)

    gate = acc[pl.ds(0, units), :]
    up = acc[pl.ds(units, units), :]
    down = pltpu.roll(acc[pl.ds(2 * units, units), :], wide - CAPACITY, 1)
    lane = lax.broadcasted_iota(jnp.int32, (units, wide), 1)
    is_x = jnp.bitwise_and(lane, 2 * CAPACITY - 1) < CAPACITY
    sig = jax.nn.sigmoid(gate)
    act = gate * sig
    d_gate = down * up * sig * (1.0 + gate * (1.0 - sig))
    d_up = down * act
    hidden = pltpu.roll(jnp.where(is_x, act * up, 0.0), CAPACITY, 1)
    sides[pl.ds(0, units), :] = jnp.where(is_x, d_gate, 0.0).astype(jnp.bfloat16)
    sides[pl.ds(units, units), :] = jnp.where(is_x, d_up, 0.0).astype(jnp.bfloat16)
    sides[pl.ds(2 * units, units), :] = hidden.astype(jnp.bfloat16)

    row = lax.broadcasted_iota(jnp.int32, (rows, wide), 0)
    col = lax.broadcasted_iota(jnp.int32, (rows, wide), 1)
    slot = (row // CAPACITY) * (2 * CAPACITY) + jnp.bitwise_and(row, CAPACITY - 1)
    compact = (slot == col).astype(jnp.float32).astype(jnp.bfloat16)
    d_rows = dot(compact, sides[pl.ds(0, 2 * units), :], NT).astype(jnp.bfloat16)

    def quarter(dx):
        block = lax.rem(x + dx, SIDE)
        cols = pl.ds(pl.multiple_of(block * (SIDE * LANES), LANES), SIDE * LANES)
        value = dot(d_rows, w[pl.ds(0, 2 * units), cols], NN).astype(jnp.bfloat16)
        for j in range(SIDE):
            p[block * SIDE + j] = value[:, j * LANES : (j + 1) * LANES]
        return block * SIDE

    for load in loads[3:]:
        load.wait()
    swaps, kept = [], []

    def fresh(i):
        span = pl.ds(i * units, units)
        for k in range(SIDE * SIDE // 2):
            rhs = jnp.concatenate(
                [g[2 * k].reshape(wide, LANES), g[2 * k + 1].reshape(wide, LANES)], axis=1
            )
            grad = dot(sides[span, :], rhs, NN)
            cols = pl.ds(2 * k * LANES, 2 * LANES)
            old = m[span, cols].astype(jnp.float32)
            own[span, cols] = (MOMENT_DECAY * old + (1.0 - MOMENT_DECAY) * grad).astype(
                jnp.bfloat16
            )
        copy = pltpu.make_async_copy(own.at[span], own_ref.at[span], own_sem.at[i])
        copy.start()
        kept.append(copy)

    def swap(i):
        span = pl.ds(i * (units // 2), units // 2)
        swaps.append(push(own.at[span], got_ref.at[span], (ms_sem, mr_sem), i, partner))

    ps = (ps_sem, pr_sem)
    o = quarter(2)
    from_a = push(p.at[pl.ds(o, 2)], buf_a, ps, 0, x_right)
    from_b = push(p.at[pl.ds(o + 2, 2)], buf_b, ps, 1, x_left)
    fresh(0)
    swap(0)
    swap(1)
    r = quarter(1)
    c_high = push(p.at[pl.ds(r + 2, 2)], buf_c.at[pl.ds(2, 2)], ps, 2, x_right)
    l = quarter(3)
    d_low = push(p.at[pl.ds(l, 2)], buf_d.at[pl.ds(0, 2)], ps, 3, x_left)
    fresh(1)
    swap(2)
    s = quarter(0)

    def add(a, b):
        return (a.astype(jnp.float32) + b.astype(jnp.float32)).astype(jnp.bfloat16)

    from_a.wait_recv()
    tmp_r[...] = add(p[pl.ds(r, 2)], buf_a[...])
    c_low = push(tmp_r, buf_c.at[pl.ds(0, 2)], ps, 4, x_right)
    from_b.wait_recv()
    tmp_l[...] = add(p[pl.ds(l + 2, 2)], buf_b[...])
    d_high = push(tmp_l, buf_d.at[pl.ds(2, 2)], ps, 5, x_left)
    for copy in (c_high, d_low, c_low, d_high):
        copy.wait_recv()
    q[...] = (
        p[pl.ds(s, SIDE)].astype(f32) + buf_c[...].astype(f32) + buf_d[...].astype(f32)
    ).astype(jnp.bfloat16)

    top, low_rows = pl.ds(0, rows // 2), pl.ds(rows // 2, rows // 2)
    yo, yr, yl = lax.rem(y + 2, SIDE), lax.rem(y + 1, SIDE), lax.rem(y + 3, SIDE)
    from_a = push(q.at[yo, top], y_a, ps, 6, y_right)
    from_b = push(q.at[yo, low_rows], y_b, ps, 7, y_left)
    c_high = push(q.at[yr, low_rows], y_c.at[low_rows], ps, 8, y_right)
    d_low = push(q.at[yl, top], y_d.at[top], ps, 9, y_left)
    swap(3)
    fresh(2)
    from_a.wait_recv()
    y_r[...] = add(q[yr, top], y_a[...])
    c_low = push(y_r, y_c.at[top], ps, 10, y_right)
    from_b.wait_recv()
    y_l[...] = add(q[yl, low_rows], y_b[...])
    d_high = push(y_l, y_d.at[low_rows], ps, 11, y_left)
    swap(4)
    for copy in (c_high, d_low, c_low, d_high):
        copy.wait_recv()
    total = (q[y].astype(f32) + y_c[...].astype(f32) + y_d[...].astype(f32)).astype(jnp.bfloat16)

    row = lax.broadcasted_iota(jnp.int32, (wide, rows), 0)
    col = lax.broadcasted_iota(jnp.int32, (wide, rows), 1)
    slot = (col // CAPACITY) * (2 * CAPACITY) + jnp.bitwise_and(col, CAPACITY - 1)
    spread = (slot == row).astype(jnp.float32).astype(jnp.bfloat16)
    back[...] = dot(spread, total, NN).astype(jnp.bfloat16).reshape(back.shape)

    def give(i, carry):
        to = peer(count - i, 0, 0)
        remote(back.at[i], ret.at[e], ret_sem.at[0], ret_sem.at[1], to).start()
        return carry

    lax.fori_loop(1, count, give, 0)
    swap(5)
    keep = pltpu.make_async_copy(back.at[0], ret.at[e], ret_sem.at[2])
    keep.start()
    keep.wait()
    given = remote(
        back.at[pl.ds(0, count - 1)],
        ret.at[pl.ds(0, count - 1)],
        ret_sem.at[0],
        ret_sem.at[1],
        x_right,
    )
    given.wait_recv()
    tok_ref[...] = dot(collect[...], ret[...].reshape(wide, LANES), TN).astype(jnp.bfloat16)

    for copy in swaps:
        copy.wait_recv()
    for copy in sent:
        copy.wait_send()
    dealt(1, count - 1, 1).wait_send()
    given.wait_send()
    for copy in kept:
        copy.wait()


def run_kernel(small, weights, moments):
    ids, _, tokens, _, relocate = small
    count = relocate.shape[1]
    tok_rows = tokens.shape[0]
    units, width = weights[0].shape
    wide, rows = count * 2 * CAPACITY, count * CAPACITY
    blocks = SIDE * SIDE
    bf16, f32 = jnp.bfloat16, jnp.float32
    vmem, dma = pltpu.VMEM, pltpu.SemaphoreType.DMA
    return pl.pallas_call(
        kernel,
        out_shape=(
            jax.ShapeDtypeStruct((tok_rows, LANES), bf16),
            jax.ShapeDtypeStruct((1, width), f32),
            jax.ShapeDtypeStruct((3 * units, width), bf16),
            jax.ShapeDtypeStruct((3 * units, width), bf16),
        ),
        in_specs=[pl.BlockSpec(memory_space=pl.ANY)] * 11,
        out_specs=(
            pl.BlockSpec(memory_space=vmem),
            pl.BlockSpec(memory_space=vmem),
            pl.BlockSpec(memory_space=pl.ANY),
            pl.BlockSpec(memory_space=pl.ANY),
        ),
        scratch_shapes=[
            vmem(ids.shape, jnp.int32),
            vmem(ids.shape, f32),
            vmem(tokens.shape, bf16),
            vmem(tokens.shape, bf16),
            vmem(relocate.shape, jnp.int32),
            vmem((count, 2 * CAPACITY, LANES), bf16),
            vmem((wide, tok_rows), bf16),
            vmem((3 * units, width), bf16),
            vmem((3 * units, width), bf16),
            vmem((3 * units, width), bf16),
            vmem((blocks, count, 2 * CAPACITY, LANES), bf16),
            vmem((3 * units, wide), f32),
            vmem((3 * units, wide), bf16),
            vmem((blocks, rows, LANES), bf16),
            vmem((2, rows, LANES), bf16),
            vmem((2, rows, LANES), bf16),
            vmem((4, rows, LANES), bf16),
            vmem((4, rows, LANES), bf16),
            vmem((2, rows, LANES), bf16),
            vmem((2, rows, LANES), bf16),
            vmem((4, rows, LANES), bf16),
            vmem((rows // 2, LANES), bf16),
            vmem((rows // 2, LANES), bf16),
            vmem((rows, LANES), bf16),
            vmem((rows, LANES), bf16),
            vmem((rows // 2, LANES), bf16),
            vmem((rows // 2, LANES), bf16),
            vmem((count, 2 * CAPACITY, LANES), bf16),
            vmem((count, 2 * CAPACITY, LANES), bf16),
            dma((11,)),
            dma((4,)),
            dma((40,)),
            dma((40,)),
            dma((12,)),
            dma((12,)),
            dma((6,)),
            dma((6,)),
            dma((3,)),
            dma((3,)),
        ],
        compiler_params=pltpu.CompilerParams(
            collective_id=0, has_side_effects=True, vmem_limit_bytes=67043328
        ),
        name="experts",
    )(*small, *weights, *moments)


def on_device(
    tokens,
    out_cotangent,
    expert_ids,
    gate_probs,
    relocate,
    w_gate,
    w_up,
    w_down,
    moment_gate,
    moment_up,
    moment_down,
):
    token_grad, flag, own, got = run_kernel(
        (expert_ids.T, gate_probs.T, tokens, out_cotangent, relocate[None]),
        (w_gate[0].T, w_up[0].T, w_down[0]),
        (moment_gate[0].T, moment_up[0].T, moment_down[0]),
    )
    units = w_down.shape[1]
    fresh = [
        jnp.where(flag == 1.0, got[i * units : (i + 1) * units], own[i * units : (i + 1) * units])
        for i in range(3)
    ]
    return (token_grad, fresh[0].T[None], fresh[1].T[None], fresh[2][None])


def solution(mesh):
    return jax.shard_map(
        on_device,
        mesh=mesh,
        in_specs=(
            P("expert", "hidden"),
            P("expert", "hidden"),
            P("expert", None),
            P("expert", None),
            P(),
            P("expert", None, "hidden"),
            P("expert", None, "hidden"),
            P("expert", "hidden", None),
            P("expert", None, "hidden"),
            P("expert", None, "hidden"),
            P("expert", "hidden", None),
        ),
        out_specs=(
            P("expert", "hidden"),
            P("expert", None, "hidden"),
            P("expert", None, "hidden"),
            P("expert", "hidden", None),
        ),
        check_vma=False,
    )
```

```python
import functools

import jax
import jax.numpy as jnp
from jax import lax
from jax.experimental import pallas as pl
from jax.experimental.pallas import tpu as pltpu
from jax.sharding import PartitionSpec as P

MOMENT_DECAY = 0.9
CAPACITY = 4
LANES = 128
SIDE = 4
MESH = pl.DeviceIdType.MESH
NT = (((1,), (1,)), ((), ()))
NN = (((1,), (0,)), ((), ()))
TN = (((0,), (0,)), ((), ()))


def dot(a, b, dims):
    return lax.dot_general(a, b, dims, preferred_element_type=jnp.float32)


def kernel(
    ids_ref,
    probs_ref,
    tokens_ref,
    cot_ref,
    relocate_ref,
    wg_ref,
    wu_ref,
    wd_ref,
    mg_ref,
    mu_ref,
    md_ref,
    tok_ref,
    new_gate_ref,
    new_up_ref,
    new_down_ref,
    ids,
    probs,
    toks,
    cots,
    moved,
    send,
    collect,
    own,
    got,
    new,
    w,
    m,
    g,
    acc,
    sides,
    p,
    buf_a,
    buf_b,
    buf_c,
    buf_d,
    tmp_r,
    tmp_l,
    q,
    y_a,
    y_b,
    y_c,
    y_d,
    y_r,
    y_l,
    back,
    ret,
    load_sem,
    a2a_sem,
    gs_sem,
    gr_sem,
    ps_sem,
    pr_sem,
    ms_sem,
    mr_sem,
    ret_sem,
    own_sem,
):
    count = send.shape[0]
    units = wg_ref.shape[0]
    tok_rows = tokens_ref.shape[0]
    wide = count * 2 * CAPACITY
    rows = count * CAPACITY
    half = count // 2
    e = lax.axis_index("expert")
    hid = lax.axis_index("hidden")
    x, y = lax.div(hid, SIDE), lax.rem(hid, SIDE)

    def h_at(dx, dy):
        return lax.rem(x + dx, SIDE) * SIDE + lax.rem(y + dy, SIDE)

    def peer(de, dx, dy):
        return (lax.rem(e + de, count), h_at(dx, dy))

    x_right, x_left = peer(0, 1, 0), peer(0, 3, 0)
    y_right, y_left = peer(0, 0, 1), peer(0, 0, 3)
    partner = peer(half, 0, 0)

    small = [
        pltpu.make_async_copy(src, dst, load_sem.at[6 + i])
        for i, (src, dst) in enumerate(
            (
                (ids_ref, ids),
                (probs_ref, probs),
                (tokens_ref, toks),
                (cot_ref, cots),
                (relocate_ref, moved),
            )
        )
    ]
    for load in small:
        load.start()
    loads = [
        pltpu.make_async_copy(src, dst.at[pl.ds(i * units, units)], load_sem.at[j * 3 + i])
        for j, (dst, group) in enumerate(
            ((w, (wg_ref, wu_ref, wd_ref)), (m, (mg_ref, mu_ref, md_ref)))
        )
        for i, src in enumerate(group)
    ]
    for load in loads:
        load.start()

    barrier = pltpu.get_barrier_semaphore()

    def far_first(act):
        def near(k, carry):
            act(half // 2 + lax.div(k + 1, 2) * (1 - 2 * lax.rem(k, 2)))
            return carry

        def across(k, carry):
            act(half + half // 2 + lax.div(k + 1, 2) * (1 - 2 * lax.rem(k, 2)))
            return carry

        lax.fori_loop(0, half - 1, near, 0)
        lax.fori_loop(0, half, across, 0)

    def greet(i):
        pl.semaphore_signal(barrier, inc=1, device_id=peer(i, 0, 0), device_id_type=MESH)

    far_first(greet)
    for near in (x_right, x_left, y_right, y_left):
        pl.semaphore_signal(barrier, inc=1, device_id=near, device_id_type=MESH)

    for load in small:
        load.wait()
    f32, bf16 = jnp.float32, jnp.bfloat16
    slot = lax.broadcasted_iota(jnp.int32, (wide, tok_rows), 0)
    expert = slot // (2 * CAPACITY)
    place = jnp.bitwise_and(slot, 2 * CAPACITY - 1)
    named = jnp.zeros((wide, tok_rows), f32)
    scale = jnp.zeros((wide, tok_rows), f32)
    for k in range(ids_ref.shape[0]):
        hit = expert == ids[k : k + 1, :]
        named += jnp.where(hit, 1.0, 0.0)
        scale += jnp.where(hit, probs[k : k + 1, :], 0.0)
    earlier = lax.broadcasted_iota(jnp.int32, (tok_rows, tok_rows), 0)
    later = lax.broadcasted_iota(jnp.int32, (tok_rows, tok_rows), 1)
    before = jnp.where(earlier < later, 1.0, 0.0).astype(bf16)
    rank = dot(named.astype(bf16), before, NN)
    want = jnp.bitwise_and(place, CAPACITY - 1).astype(f32)
    chosen = jnp.where(rank == want, named, 0.0)
    take_x = jnp.where(place < CAPACITY, chosen, 0.0).astype(bf16)
    scale = jnp.where(place < CAPACITY, 0.0, chosen * scale)
    collect[...] = take_x
    dealing = dot(take_x, toks[...], NN)
    for _ in range(3):
        part = scale.astype(bf16)
        dealing += dot(part, cots[...], NN)
        scale = scale - part.astype(f32)
    send[...] = dealing.astype(bf16).reshape(send.shape)
    lanes = lax.broadcasted_iota(jnp.int32, moved.shape, 1)
    flag = jnp.sum(jnp.where(lanes == e, moved[...], 0), axis=1, keepdims=True)
    pl.semaphore_wait(barrier, count - 1 + 4)

    def remote(src, dst, ssem, rsem, to):
        return pltpu.make_async_remote_copy(
            src_ref=src,
            dst_ref=dst,
            send_sem=ssem,
            recv_sem=rsem,
            device_id=to,
            device_id_type=MESH,
        )

    me = h_at(0, 0)

    quart = half // 2
    sizes = (half, quart, quart)
    starts = (0, half, half + quart)
    streams = (0, 1, 2)

    def deal(i):
        to = peer(i, 0, 0)
        n = 1 + lax.div(i, half) + lax.div(i, half + quart)
        remote(send.at[to[0]], g.at[me, i], a2a_sem.at[0], a2a_sem.at[n], to).start()

    far_first(deal)
    keep = pltpu.make_async_copy(send.at[e], g.at[me, 0], a2a_sem.at[4])
    keep.start()

    def dealt(first, size, n):
        span = pl.ds(first, size)
        return remote(send.at[span], g.at[me, span], a2a_sem.at[0], a2a_sem.at[n], x_right)

    sent = []

    def push(src, dst, sems, n, to):
        copy = remote(src, dst, sems[0].at[n], sems[1].at[n], to)
        copy.start()
        sent.append(copy)
        return copy

    gs = (gs_sem, gr_sem)

    def block(c, second, first):
        return h_at(second, first) if c < 2 else h_at(first, second)

    def sides_of(c, stage):
        return (y_right, y_left) if (stage == 0) == (c < 2) else (x_right, x_left)

    def part(h, c):
        return g.at[h, pl.ds(starts[c], sizes[c])]

    def low(h, c):
        return g.at[h, pl.ds(starts[c], sizes[c] // 2)]

    def high(h, c):
        return g.at[h, pl.ds(starts[c] + sizes[c] // 2, sizes[c] // 2)]

    def out(n, h, c, stage):
        src = part(h, c)
        right, left = sides_of(c, stage)
        n = 20 * c + n
        return push(src, src, gs, n, right), push(src, src, gs, n + 1, left)

    def forward(n, c, left_h, right_h, arrivals, stage):
        right, left = sides_of(c, stage)
        n = 20 * c + n
        arrivals[0].wait_recv()
        a = low(left_h, c)
        a = push(a, a, gs, n, right)
        arrivals[1].wait_recv()
        b = high(right_h, c)
        return a, push(b, b, gs, n + 1, left)

    order = (0, 3, 1, 2)

    def second_out(b, c):
        return out(4 + 4 * order.index(b), block(c, 0, b), c, 1)

    def second_forward(b, c):
        n = 6 + 4 * order.index(b)
        fwd[c, b] = forward(n, c, block(c, 3, b), block(c, 1, b), into[c, b], 1)

    def absorb(a, b, c, begins=False):
        h = block(c, a, b)
        cols = pl.ds(pl.multiple_of(h * LANES, LANES), LANES)
        wide_c = sizes[c] * 2 * CAPACITY
        mine = pl.ds(starts[c] * 2 * CAPACITY, wide_c)
        term = dot(w[:, cols], part(h, c)[...].reshape(wide_c, LANES), NT)
        if begins:
            acc[:, mine] = term
        else:
            acc[:, mine] += term

    first_in, into, fwd, opp = {}, {}, {}, {}

    def begin(c):
        first_in[c] = out(0, me, c, 0)
        into[c, 0] = second_out(0, c)

    keep.wait()
    dealt(1, half - 1, 1).wait_recv()
    begin(0)
    for load in loads[:3]:
        load.wait()
    absorb(0, 0, 0, True)
    for c in (1, 2):
        dealt(starts[c], sizes[c], c + 1).wait_recv()
        begin(c)
    for c in (1, 2):
        absorb(0, 0, c, True)
    for c in streams:
        opp[c] = forward(2, c, block(c, 0, 3), block(c, 0, 1), first_in[c], 0)
        into[c, 3] = second_out(3, c)
        into[c, 1] = second_out(1, c)
        second_forward(0, c)
    for c in streams:
        absorb(0, 3, c)
        absorb(0, 1, c)
        absorb(3, 0, c)
        absorb(1, 0, c)
    for c in streams:
        for copy in opp[c]:
            copy.wait_recv()
        into[c, 2] = second_out(2, c)
        second_forward(3, c)
    for c in streams:
        absorb(0, 2, c)
        absorb(3, 3, c)
        absorb(1, 3, c)

    def finish(c, b):
        for copy in fwd[c, b]:
            copy.wait_recv()
        absorb(2, b, c)

    for c in streams:
        second_forward(1, c)
        absorb(3, 1, c)
        absorb(1, 1, c)
    for c in streams:
        finish(c, 0)
        second_forward(2, c)
        absorb(3, 2, c)
        absorb(1, 2, c)
    for b in (3, 1, 2):
        for c in streams:
            finish(c, b)

    gate = acc[pl.ds(0, units), :]
    up = acc[pl.ds(units, units), :]
    down = pltpu.roll(acc[pl.ds(2 * units, units), :], wide - CAPACITY, 1)
    lane = lax.broadcasted_iota(jnp.int32, (units, wide), 1)
    is_x = jnp.bitwise_and(lane, 2 * CAPACITY - 1) < CAPACITY
    sig = jax.nn.sigmoid(gate)
    act = gate * sig
    d_gate = down * up * sig * (1.0 + gate * (1.0 - sig))
    d_up = down * act
    hidden = pltpu.roll(jnp.where(is_x, act * up, 0.0), CAPACITY, 1)
    sides[pl.ds(0, units), :] = jnp.where(is_x, d_gate, 0.0).astype(jnp.bfloat16)
    sides[pl.ds(units, units), :] = jnp.where(is_x, d_up, 0.0).astype(jnp.bfloat16)
    sides[pl.ds(2 * units, units), :] = hidden.astype(jnp.bfloat16)

    row = lax.broadcasted_iota(jnp.int32, (rows, wide), 0)
    col = lax.broadcasted_iota(jnp.int32, (rows, wide), 1)
    slot = (row // CAPACITY) * (2 * CAPACITY) + jnp.bitwise_and(row, CAPACITY - 1)
    compact = (slot == col).astype(jnp.float32).astype(jnp.bfloat16)
    d_rows = dot(compact, sides[pl.ds(0, 2 * units), :], NT).astype(jnp.bfloat16)

    def quarter(dx):
        block = lax.rem(x + dx, SIDE)
        cols = pl.ds(pl.multiple_of(block * (SIDE * LANES), LANES), SIDE * LANES)
        value = dot(d_rows, w[pl.ds(0, 2 * units), cols], NN).astype(jnp.bfloat16)
        for j in range(SIDE):
            p[block * SIDE + j] = value[:, j * LANES : (j + 1) * LANES]
        return block * SIDE

    for load in loads[3:]:
        load.wait()
    swaps, kept = {}, []

    def fresh(i):
        span = pl.ds(i * units, units)
        for k in range(SIDE * SIDE // 2):
            rhs = jnp.concatenate(
                [g[2 * k].reshape(wide, LANES), g[2 * k + 1].reshape(wide, LANES)], axis=1
            )
            grad = dot(sides[span, :], rhs, NN)
            cols = pl.ds(2 * k * LANES, 2 * LANES)
            old = m[span, cols].astype(jnp.float32)
            own[span, cols] = (MOMENT_DECAY * old + (1.0 - MOMENT_DECAY) * grad).astype(
                jnp.bfloat16
            )

    def swap(i):
        span = pl.ds(i * (units // 2), units // 2)
        swaps[i] = push(own.at[span], got.at[span], (ms_sem, mr_sem), i, partner)

    def land(i):
        for j in (2 * i, 2 * i + 1):
            swaps[j].wait_recv()
            span = pl.ds(j * (units // 2), units // 2)
            moves = jnp.broadcast_to(flag, (units // 2, got.shape[1])) == 1
            new[span, :] = jnp.where(
                moves, got[span, :].astype(f32), own[span, :].astype(f32)
            ).astype(bf16)
        span = pl.ds(i * units, units)
        target = (new_gate_ref, new_up_ref, new_down_ref)[i]
        copy = pltpu.make_async_copy(new.at[span], target, own_sem.at[i])
        copy.start()
        kept.append(copy)

    ps = (ps_sem, pr_sem)
    o = quarter(2)
    from_a = push(p.at[pl.ds(o, 2)], buf_a, ps, 0, x_right)
    from_b = push(p.at[pl.ds(o + 2, 2)], buf_b, ps, 1, x_left)
    fresh(0)
    swap(0)
    swap(1)
    r = quarter(1)
    c_high = push(p.at[pl.ds(r + 2, 2)], buf_c.at[pl.ds(2, 2)], ps, 2, x_right)
    l = quarter(3)
    d_low = push(p.at[pl.ds(l, 2)], buf_d.at[pl.ds(0, 2)], ps, 3, x_left)
    fresh(1)
    swap(2)
    s = quarter(0)

    def add(a, b):
        return (a.astype(jnp.float32) + b.astype(jnp.float32)).astype(jnp.bfloat16)

    from_a.wait_recv()
    tmp_r[...] = add(p[pl.ds(r, 2)], buf_a[...])
    c_low = push(tmp_r, buf_c.at[pl.ds(0, 2)], ps, 4, x_right)
    from_b.wait_recv()
    tmp_l[...] = add(p[pl.ds(l + 2, 2)], buf_b[...])
    d_high = push(tmp_l, buf_d.at[pl.ds(2, 2)], ps, 5, x_left)
    for copy in (c_high, d_low, c_low, d_high):
        copy.wait_recv()
    q[...] = (
        p[pl.ds(s, SIDE)].astype(f32) + buf_c[...].astype(f32) + buf_d[...].astype(f32)
    ).astype(jnp.bfloat16)

    top, low_rows = pl.ds(0, rows // 2), pl.ds(rows // 2, rows // 2)
    yo, yr, yl = lax.rem(y + 2, SIDE), lax.rem(y + 1, SIDE), lax.rem(y + 3, SIDE)
    from_a = push(q.at[yo, top], y_a, ps, 6, y_right)
    from_b = push(q.at[yo, low_rows], y_b, ps, 7, y_left)
    c_high = push(q.at[yr, low_rows], y_c.at[low_rows], ps, 8, y_right)
    d_low = push(q.at[yl, top], y_d.at[top], ps, 9, y_left)
    swap(3)
    fresh(2)
    from_a.wait_recv()
    y_r[...] = add(q[yr, top], y_a[...])
    c_low = push(y_r, y_c.at[top], ps, 10, y_right)
    from_b.wait_recv()
    y_l[...] = add(q[yl, low_rows], y_b[...])
    d_high = push(y_l, y_d.at[low_rows], ps, 11, y_left)
    swap(4)
    for copy in (c_high, d_low, c_low, d_high):
        copy.wait_recv()
    total = (q[y].astype(f32) + y_c[...].astype(f32) + y_d[...].astype(f32)).astype(jnp.bfloat16)

    row = lax.broadcasted_iota(jnp.int32, (wide, rows), 0)
    col = lax.broadcasted_iota(jnp.int32, (wide, rows), 1)
    slot = (col // CAPACITY) * (2 * CAPACITY) + jnp.bitwise_and(col, CAPACITY - 1)
    spread = (slot == row).astype(jnp.float32).astype(jnp.bfloat16)
    back[...] = dot(spread, total, NN).astype(jnp.bfloat16).reshape(back.shape)

    def give(i):
        to = peer(count - i, 0, 0)
        remote(back.at[i], ret.at[e], ret_sem.at[0], ret_sem.at[1], to).start()

    far_first(give)
    swap(5)
    keep = pltpu.make_async_copy(back.at[0], ret.at[e], ret_sem.at[2])
    keep.start()
    keep.wait()
    given = remote(
        back.at[pl.ds(0, count - 1)],
        ret.at[pl.ds(0, count - 1)],
        ret_sem.at[0],
        ret_sem.at[1],
        x_right,
    )
    land(0)
    given.wait_recv()
    tok_ref[...] = dot(collect[...], ret[...].reshape(wide, LANES), TN).astype(jnp.bfloat16)

    land(1)
    land(2)
    for copy in sent:
        copy.wait_send()
    dealt(1, count - 1, 1).wait_send()
    given.wait_send()
    for copy in kept:
        copy.wait()


def run_kernel(small, weights, moments):
    ids, _, tokens, _, relocate = small
    count = relocate.shape[1]
    tok_rows = tokens.shape[0]
    units, width = weights[0].shape
    wide, rows = count * 2 * CAPACITY, count * CAPACITY
    blocks = SIDE * SIDE
    bf16, f32 = jnp.bfloat16, jnp.float32
    vmem, dma = pltpu.VMEM, pltpu.SemaphoreType.DMA
    return pl.pallas_call(
        kernel,
        out_shape=(
            jax.ShapeDtypeStruct((tok_rows, LANES), bf16),
            jax.ShapeDtypeStruct((units, width), bf16),
            jax.ShapeDtypeStruct((units, width), bf16),
            jax.ShapeDtypeStruct((units, width), bf16),
        ),
        in_specs=[pl.BlockSpec(memory_space=pl.ANY)] * 11,
        out_specs=(
            pl.BlockSpec(memory_space=vmem),
            pl.BlockSpec(memory_space=pl.ANY),
            pl.BlockSpec(memory_space=pl.ANY),
            pl.BlockSpec(memory_space=pl.ANY),
        ),
        scratch_shapes=[
            vmem(ids.shape, jnp.int32),
            vmem(ids.shape, f32),
            vmem(tokens.shape, bf16),
            vmem(tokens.shape, bf16),
            vmem(relocate.shape, jnp.int32),
            vmem((count, 2 * CAPACITY, LANES), bf16),
            vmem((wide, tok_rows), bf16),
            vmem((3 * units, width), bf16),
            vmem((3 * units, width), bf16),
            vmem((3 * units, width), bf16),
            vmem((3 * units, width), bf16),
            vmem((3 * units, width), bf16),
            vmem((blocks, count, 2 * CAPACITY, LANES), bf16),
            vmem((3 * units, wide), f32),
            vmem((3 * units, wide), bf16),
            vmem((blocks, rows, LANES), bf16),
            vmem((2, rows, LANES), bf16),
            vmem((2, rows, LANES), bf16),
            vmem((4, rows, LANES), bf16),
            vmem((4, rows, LANES), bf16),
            vmem((2, rows, LANES), bf16),
            vmem((2, rows, LANES), bf16),
            vmem((4, rows, LANES), bf16),
            vmem((rows // 2, LANES), bf16),
            vmem((rows // 2, LANES), bf16),
            vmem((rows, LANES), bf16),
            vmem((rows, LANES), bf16),
            vmem((rows // 2, LANES), bf16),
            vmem((rows // 2, LANES), bf16),
            vmem((count, 2 * CAPACITY, LANES), bf16),
            vmem((count, 2 * CAPACITY, LANES), bf16),
            dma((11,)),
            dma((5,)),
            dma((60,)),
            dma((60,)),
            dma((12,)),
            dma((12,)),
            dma((6,)),
            dma((6,)),
            dma((3,)),
            dma((3,)),
        ],
        compiler_params=pltpu.CompilerParams(
            collective_id=0, has_side_effects=True, vmem_limit_bytes=67043328
        ),
        name="experts",
    )(*small, *weights, *moments)


def on_device(
    tokens,
    out_cotangent,
    expert_ids,
    gate_probs,
    relocate,
    w_gate,
    w_up,
    w_down,
    moment_gate,
    moment_up,
    moment_down,
):
    token_grad, new_gate, new_up, new_down = run_kernel(
        (expert_ids.T, gate_probs.T, tokens, out_cotangent, relocate[None]),
        (w_gate[0].T, w_up[0].T, w_down[0]),
        (moment_gate[0].T, moment_up[0].T, moment_down[0]),
    )
    return (token_grad, new_gate.T[None], new_up.T[None], new_down[None])


def solution(mesh):
    return jax.shard_map(
        on_device,
        mesh=mesh,
        in_specs=(
            P("expert", "hidden"),
            P("expert", "hidden"),
            P("expert", None),
            P("expert", None),
            P(),
            P("expert", None, "hidden"),
            P("expert", None, "hidden"),
            P("expert", "hidden", None),
            P("expert", None, "hidden"),
            P("expert", None, "hidden"),
            P("expert", "hidden", None),
        ),
        out_specs=(
            P("expert", "hidden"),
            P("expert", None, "hidden"),
            P("expert", None, "hidden"),
            P("expert", "hidden", None),
        ),
        check_vma=False,
    )
```

```python
import functools

import jax
import jax.numpy as jnp
from jax import lax
from jax.experimental import pallas as pl
from jax.experimental.pallas import tpu as pltpu
from jax.sharding import PartitionSpec as P

MOMENT_DECAY = 0.9
CAPACITY = 4
LANES = 128
SIDE = 4
MESH = pl.DeviceIdType.MESH
NT = (((1,), (1,)), ((), ()))
NN = (((1,), (0,)), ((), ()))
TN = (((0,), (0,)), ((), ()))


def dot(a, b, dims):
    return lax.dot_general(a, b, dims, preferred_element_type=jnp.float32)


def kernel(
    ids_ref,
    probs_ref,
    tokens_ref,
    cot_ref,
    relocate_ref,
    wg_ref,
    wu_ref,
    wd_ref,
    mg_ref,
    mu_ref,
    md_ref,
    tok_ref,
    new_ref,
    ids,
    probs,
    toks,
    cots,
    moved,
    send,
    collect,
    own,
    got,
    new,
    w,
    m,
    g,
    acc,
    sides,
    p,
    buf_a,
    buf_b,
    buf_c,
    buf_d,
    tmp_r,
    tmp_l,
    q,
    y_a,
    y_b,
    y_c,
    y_d,
    y_r,
    y_l,
    back,
    ret,
    load_sem,
    a2a_sem,
    gs_sem,
    gr_sem,
    ps_sem,
    pr_sem,
    ms_sem,
    mr_sem,
    ret_sem,
    own_sem,
):
    count = send.shape[0]
    units = wg_ref.shape[0]
    tok_rows = tokens_ref.shape[0]
    wide = count * 2 * CAPACITY
    rows = count * CAPACITY
    half = count // 2
    e = lax.axis_index("expert")
    hid = lax.axis_index("hidden")
    x, y = lax.div(hid, SIDE), lax.rem(hid, SIDE)

    def h_at(dx, dy):
        return lax.rem(x + dx, SIDE) * SIDE + lax.rem(y + dy, SIDE)

    def peer(de, dx, dy):
        return (lax.rem(e + de, count), h_at(dx, dy))

    x_right, x_left = peer(0, 1, 0), peer(0, 3, 0)
    y_right, y_left = peer(0, 0, 1), peer(0, 0, 3)
    partner = peer(half, 0, 0)

    small = [
        pltpu.make_async_copy(src, dst, load_sem.at[6 + i])
        for i, (src, dst) in enumerate(
            (
                (ids_ref, ids),
                (probs_ref, probs),
                (tokens_ref, toks),
                (cot_ref, cots),
                (relocate_ref, moved),
            )
        )
    ]
    for load in small:
        load.start()
    loads = [
        pltpu.make_async_copy(src, dst.at[pl.ds(i * units, units)], load_sem.at[j * 3 + i])
        for j, (dst, group) in enumerate(
            ((w, (wg_ref, wu_ref, wd_ref)), (m, (mg_ref, mu_ref, md_ref)))
        )
        for i, src in enumerate(group)
    ]
    for load in loads:
        load.start()

    barrier = pltpu.get_barrier_semaphore()

    def in_order(act):
        def step(i, carry):
            act(i)
            return carry

        lax.fori_loop(1, count, step, 0)

    def greet(i):
        pl.semaphore_signal(barrier, inc=1, device_id=peer(i, 0, 0), device_id_type=MESH)

    in_order(greet)
    for near in (x_right, x_left, y_right, y_left):
        pl.semaphore_signal(barrier, inc=1, device_id=near, device_id_type=MESH)

    for load in small:
        load.wait()
    f32, bf16 = jnp.float32, jnp.bfloat16
    slot = lax.broadcasted_iota(jnp.int32, (wide, tok_rows), 0)
    expert = slot // (2 * CAPACITY)
    place = jnp.bitwise_and(slot, 2 * CAPACITY - 1)
    named = jnp.zeros((wide, tok_rows), f32)
    scale = jnp.zeros((wide, tok_rows), f32)
    for k in range(ids_ref.shape[0]):
        hit = expert == ids[k : k + 1, :]
        named += jnp.where(hit, 1.0, 0.0)
        scale += jnp.where(hit, probs[k : k + 1, :], 0.0)
    earlier = lax.broadcasted_iota(jnp.int32, (tok_rows, tok_rows), 0)
    later = lax.broadcasted_iota(jnp.int32, (tok_rows, tok_rows), 1)
    before = jnp.where(earlier < later, 1.0, 0.0).astype(bf16)
    rank = dot(named.astype(bf16), before, NN)
    want = jnp.bitwise_and(place, CAPACITY - 1).astype(f32)
    chosen = jnp.where(rank == want, named, 0.0)
    take_x = jnp.where(place < CAPACITY, chosen, 0.0).astype(bf16)
    scale = jnp.where(place < CAPACITY, 0.0, chosen * scale)
    collect[...] = take_x
    dealing = dot(take_x, toks[...], NN)
    for _ in range(3):
        part = scale.astype(bf16)
        dealing += dot(part, cots[...], NN)
        scale = scale - part.astype(f32)
    send[...] = dealing.astype(bf16).reshape(send.shape)
    lanes = lax.broadcasted_iota(jnp.int32, moved.shape, 1)
    flag = jnp.sum(jnp.where(lanes == e, moved[...], 0), axis=1, keepdims=True)
    pl.semaphore_wait(barrier, count - 1 + 4)

    def remote(src, dst, ssem, rsem, to):
        return pltpu.make_async_remote_copy(
            src_ref=src,
            dst_ref=dst,
            send_sem=ssem,
            recv_sem=rsem,
            device_id=to,
            device_id_type=MESH,
        )

    me = h_at(0, 0)

    quart = half // 2
    sizes = (half, quart, quart)
    starts = (0, half, half + quart)
    streams = (0, 1, 2)

    def deal(i):
        to = peer(i, 0, 0)
        n = 1 + lax.div(i, half) + lax.div(i, half + quart)
        remote(send.at[to[0]], g.at[me, i], a2a_sem.at[0], a2a_sem.at[n], to).start()

    in_order(deal)
    keep = pltpu.make_async_copy(send.at[e], g.at[me, 0], a2a_sem.at[4])
    keep.start()

    def dealt(first, size, n):
        span = pl.ds(first, size)
        return remote(send.at[span], g.at[me, span], a2a_sem.at[0], a2a_sem.at[n], x_right)

    sent = []

    def push(src, dst, sems, n, to):
        copy = remote(src, dst, sems[0].at[n], sems[1].at[n], to)
        copy.start()
        sent.append(copy)
        return copy

    gs = (gs_sem, gr_sem)

    def block(c, second, first):
        return h_at(second, first) if c < 2 else h_at(first, second)

    def sides_of(c, stage):
        return (y_right, y_left) if (stage == 0) == (c < 2) else (x_right, x_left)

    def part(h, c):
        return g.at[h, pl.ds(starts[c], sizes[c])]

    def low(h, c):
        return g.at[h, pl.ds(starts[c], sizes[c] // 2)]

    def high(h, c):
        return g.at[h, pl.ds(starts[c] + sizes[c] // 2, sizes[c] // 2)]

    def out(n, h, c, stage):
        src = part(h, c)
        right, left = sides_of(c, stage)
        n = 20 * c + n
        return push(src, src, gs, n, right), push(src, src, gs, n + 1, left)

    def forward(n, c, left_h, right_h, arrivals, stage):
        right, left = sides_of(c, stage)
        n = 20 * c + n
        arrivals[0].wait_recv()
        a = low(left_h, c)
        a = push(a, a, gs, n, right)
        arrivals[1].wait_recv()
        b = high(right_h, c)
        return a, push(b, b, gs, n + 1, left)

    order = (0, 3, 1, 2)

    def second_out(b, c):
        return out(4 + 4 * order.index(b), block(c, 0, b), c, 1)

    def second_forward(b, c):
        n = 6 + 4 * order.index(b)
        fwd[c, b] = forward(n, c, block(c, 3, b), block(c, 1, b), into[c, b], 1)

    def absorb(a, b, c, begins=False):
        h = block(c, a, b)
        cols = pl.ds(pl.multiple_of(h * LANES, LANES), LANES)
        wide_c = sizes[c] * 2 * CAPACITY
        mine = pl.ds(starts[c] * 2 * CAPACITY, wide_c)
        term = dot(w[:, cols], part(h, c)[...].reshape(wide_c, LANES), NT)
        if begins:
            acc[:, mine] = term
        else:
            acc[:, mine] += term

    first_in, into, fwd, opp = {}, {}, {}, {}

    def begin(c):
        first_in[c] = out(0, me, c, 0)
        into[c, 0] = second_out(0, c)

    keep.wait()
    dealt(1, half - 1, 1).wait_recv()
    begin(0)
    for load in loads[:3]:
        load.wait()
    absorb(0, 0, 0, True)
    for c in (1, 2):
        dealt(starts[c], sizes[c], c + 1).wait_recv()
        begin(c)
    for c in (1, 2):
        absorb(0, 0, c, True)
    for c in streams:
        opp[c] = forward(2, c, block(c, 0, 3), block(c, 0, 1), first_in[c], 0)
        into[c, 3] = second_out(3, c)
        into[c, 1] = second_out(1, c)
        second_forward(0, c)
    for c in streams:
        absorb(0, 3, c)
        absorb(0, 1, c)
        absorb(3, 0, c)
        absorb(1, 0, c)
    for c in streams:
        for copy in opp[c]:
            copy.wait_recv()
        into[c, 2] = second_out(2, c)
        second_forward(3, c)
    for c in streams:
        absorb(0, 2, c)
        absorb(3, 3, c)
        absorb(1, 3, c)

    def finish(c, b):
        for copy in fwd[c, b]:
            copy.wait_recv()
        absorb(2, b, c)

    for c in streams:
        second_forward(1, c)
        absorb(3, 1, c)
        absorb(1, 1, c)
    for c in streams:
        finish(c, 0)
        second_forward(2, c)
        absorb(3, 2, c)
        absorb(1, 2, c)
    for b in (3, 1, 2):
        for c in streams:
            finish(c, b)

    gate = acc[pl.ds(0, units), :]
    up = acc[pl.ds(units, units), :]
    down = pltpu.roll(acc[pl.ds(2 * units, units), :], wide - CAPACITY, 1)
    lane = lax.broadcasted_iota(jnp.int32, (units, wide), 1)
    is_x = jnp.bitwise_and(lane, 2 * CAPACITY - 1) < CAPACITY
    sig = jax.nn.sigmoid(gate)
    act = gate * sig
    d_gate = down * up * sig * (1.0 + gate * (1.0 - sig))
    d_up = down * act
    hidden = pltpu.roll(jnp.where(is_x, act * up, 0.0), CAPACITY, 1)
    sides[pl.ds(0, units), :] = jnp.where(is_x, d_gate, 0.0).astype(jnp.bfloat16)
    sides[pl.ds(units, units), :] = jnp.where(is_x, d_up, 0.0).astype(jnp.bfloat16)
    sides[pl.ds(2 * units, units), :] = hidden.astype(jnp.bfloat16)

    row = lax.broadcasted_iota(jnp.int32, (rows, wide), 0)
    col = lax.broadcasted_iota(jnp.int32, (rows, wide), 1)
    slot = (row // CAPACITY) * (2 * CAPACITY) + jnp.bitwise_and(row, CAPACITY - 1)
    compact = (slot == col).astype(jnp.float32).astype(jnp.bfloat16)
    d_rows = dot(compact, sides[pl.ds(0, 2 * units), :], NT).astype(jnp.bfloat16)

    def quarter(dx):
        block = lax.rem(x + dx, SIDE)
        cols = pl.ds(pl.multiple_of(block * (SIDE * LANES), LANES), SIDE * LANES)
        value = dot(d_rows, w[pl.ds(0, 2 * units), cols], NN).astype(jnp.bfloat16)
        for j in range(SIDE):
            p[block * SIDE + j] = value[:, j * LANES : (j + 1) * LANES]
        return block * SIDE

    for load in loads[3:]:
        load.wait()
    swaps, kept = {}, []

    def fresh(i):
        span = pl.ds(i * units, units)
        for k in range(SIDE * SIDE // 2):
            rhs = jnp.concatenate(
                [g[2 * k].reshape(wide, LANES), g[2 * k + 1].reshape(wide, LANES)], axis=1
            )
            grad = dot(sides[span, :], rhs, NN)
            cols = pl.ds(2 * k * LANES, 2 * LANES)
            old = m[span, cols].astype(jnp.float32)
            own[span, cols] = (MOMENT_DECAY * old + (1.0 - MOMENT_DECAY) * grad).astype(
                jnp.bfloat16
            )

    def swap(i):
        span = pl.ds(i * (units // 2), units // 2)
        swaps[i] = push(own.at[span], got.at[span], (ms_sem, mr_sem), i, partner)

    def land(i):
        for j in (2 * i, 2 * i + 1):
            swaps[j].wait_recv()
            span = pl.ds(j * (units // 2), units // 2)
            moves = jnp.broadcast_to(flag, (units // 2, got.shape[1])) == 1
            new[span, :] = jnp.where(
                moves, got[span, :].astype(f32), own[span, :].astype(f32)
            ).astype(bf16)
        span = pl.ds(i * units, units)
        copy = pltpu.make_async_copy(new.at[span], new_ref.at[span], own_sem.at[i])
        copy.start()
        kept.append(copy)

    ps = (ps_sem, pr_sem)
    o = quarter(2)
    from_a = push(p.at[pl.ds(o, 2)], buf_a, ps, 0, x_right)
    from_b = push(p.at[pl.ds(o + 2, 2)], buf_b, ps, 1, x_left)
    fresh(0)
    swap(0)
    swap(1)
    r = quarter(1)
    c_high = push(p.at[pl.ds(r + 2, 2)], buf_c.at[pl.ds(2, 2)], ps, 2, x_right)
    l = quarter(3)
    d_low = push(p.at[pl.ds(l, 2)], buf_d.at[pl.ds(0, 2)], ps, 3, x_left)
    fresh(1)
    swap(2)
    s = quarter(0)

    def add(a, b):
        return (a.astype(jnp.float32) + b.astype(jnp.float32)).astype(jnp.bfloat16)

    from_a.wait_recv()
    tmp_r[...] = add(p[pl.ds(r, 2)], buf_a[...])
    c_low = push(tmp_r, buf_c.at[pl.ds(0, 2)], ps, 4, x_right)
    from_b.wait_recv()
    tmp_l[...] = add(p[pl.ds(l + 2, 2)], buf_b[...])
    d_high = push(tmp_l, buf_d.at[pl.ds(2, 2)], ps, 5, x_left)
    for copy in (c_high, d_low, c_low, d_high):
        copy.wait_recv()
    q[...] = (
        p[pl.ds(s, SIDE)].astype(f32) + buf_c[...].astype(f32) + buf_d[...].astype(f32)
    ).astype(jnp.bfloat16)

    top, low_rows = pl.ds(0, rows // 2), pl.ds(rows // 2, rows // 2)
    yo, yr, yl = lax.rem(y + 2, SIDE), lax.rem(y + 1, SIDE), lax.rem(y + 3, SIDE)
    from_a = push(q.at[yo, top], y_a, ps, 6, y_right)
    from_b = push(q.at[yo, low_rows], y_b, ps, 7, y_left)
    c_high = push(q.at[yr, low_rows], y_c.at[low_rows], ps, 8, y_right)
    d_low = push(q.at[yl, top], y_d.at[top], ps, 9, y_left)
    swap(3)
    fresh(2)
    from_a.wait_recv()
    y_r[...] = add(q[yr, top], y_a[...])
    c_low = push(y_r, y_c.at[top], ps, 10, y_right)
    from_b.wait_recv()
    y_l[...] = add(q[yl, low_rows], y_b[...])
    d_high = push(y_l, y_d.at[low_rows], ps, 11, y_left)
    swap(4)
    for copy in (c_high, d_low, c_low, d_high):
        copy.wait_recv()
    total = (q[y].astype(f32) + y_c[...].astype(f32) + y_d[...].astype(f32)).astype(jnp.bfloat16)

    row = lax.broadcasted_iota(jnp.int32, (wide, rows), 0)
    col = lax.broadcasted_iota(jnp.int32, (wide, rows), 1)
    slot = (col // CAPACITY) * (2 * CAPACITY) + jnp.bitwise_and(col, CAPACITY - 1)
    spread = (slot == row).astype(jnp.float32).astype(jnp.bfloat16)
    back[...] = dot(spread, total, NN).astype(jnp.bfloat16).reshape(back.shape)

    def give(i):
        to = peer(count - i, 0, 0)
        remote(back.at[i], ret.at[e], ret_sem.at[0], ret_sem.at[1], to).start()

    in_order(give)
    swap(5)
    keep = pltpu.make_async_copy(back.at[0], ret.at[e], ret_sem.at[2])
    keep.start()
    keep.wait()
    given = remote(
        back.at[pl.ds(0, count - 1)],
        ret.at[pl.ds(0, count - 1)],
        ret_sem.at[0],
        ret_sem.at[1],
        x_right,
    )
    land(0)
    given.wait_recv()
    tok_ref[...] = dot(collect[...], ret[...].reshape(wide, LANES), TN).astype(jnp.bfloat16)

    land(1)
    land(2)
    for copy in sent:
        copy.wait_send()
    dealt(1, count - 1, 1).wait_send()
    given.wait_send()
    for copy in kept:
        copy.wait()


def run_kernel(small, weights, moments):
    ids, _, tokens, _, relocate = small
    count = relocate.shape[1]
    tok_rows = tokens.shape[0]
    units, width = weights[0].shape
    wide, rows = count * 2 * CAPACITY, count * CAPACITY
    blocks = SIDE * SIDE
    bf16, f32 = jnp.bfloat16, jnp.float32
    vmem, dma = pltpu.VMEM, pltpu.SemaphoreType.DMA
    return pl.pallas_call(
        kernel,
        out_shape=(
            jax.ShapeDtypeStruct((tok_rows, LANES), bf16),
            jax.ShapeDtypeStruct((3 * units, width), bf16),
        ),
        in_specs=[pl.BlockSpec(memory_space=pl.ANY)] * 11,
        out_specs=(
            pl.BlockSpec(memory_space=vmem),
            pl.BlockSpec(memory_space=pl.ANY),
        ),
        scratch_shapes=[
            vmem(ids.shape, jnp.int32),
            vmem(ids.shape, f32),
            vmem(tokens.shape, bf16),
            vmem(tokens.shape, bf16),
            vmem(relocate.shape, jnp.int32),
            vmem((count, 2 * CAPACITY, LANES), bf16),
            vmem((wide, tok_rows), bf16),
            vmem((3 * units, width), bf16),
            vmem((3 * units, width), bf16),
            vmem((3 * units, width), bf16),
            vmem((3 * units, width), bf16),
            vmem((3 * units, width), bf16),
            vmem((blocks, count, 2 * CAPACITY, LANES), bf16),
            vmem((3 * units, wide), f32),
            vmem((3 * units, wide), bf16),
            vmem((blocks, rows, LANES), bf16),
            vmem((2, rows, LANES), bf16),
            vmem((2, rows, LANES), bf16),
            vmem((4, rows, LANES), bf16),
            vmem((4, rows, LANES), bf16),
            vmem((2, rows, LANES), bf16),
            vmem((2, rows, LANES), bf16),
            vmem((4, rows, LANES), bf16),
            vmem((rows // 2, LANES), bf16),
            vmem((rows // 2, LANES), bf16),
            vmem((rows, LANES), bf16),
            vmem((rows, LANES), bf16),
            vmem((rows // 2, LANES), bf16),
            vmem((rows // 2, LANES), bf16),
            vmem((count, 2 * CAPACITY, LANES), bf16),
            vmem((count, 2 * CAPACITY, LANES), bf16),
            dma((11,)),
            dma((5,)),
            dma((60,)),
            dma((60,)),
            dma((12,)),
            dma((12,)),
            dma((6,)),
            dma((6,)),
            dma((3,)),
            dma((3,)),
        ],
        compiler_params=pltpu.CompilerParams(
            collective_id=0, has_side_effects=True, vmem_limit_bytes=67043328
        ),
        name="experts",
    )(*small, *weights, *moments)


def on_device(
    tokens,
    out_cotangent,
    expert_ids,
    gate_probs,
    relocate,
    w_gate,
    w_up,
    w_down,
    moment_gate,
    moment_up,
    moment_down,
):
    token_grad, new = run_kernel(
        (expert_ids.T, gate_probs.T, tokens, out_cotangent, relocate[None]),
        (w_gate[0].T, w_up[0].T, w_down[0]),
        (moment_gate[0].T, moment_up[0].T, moment_down[0]),
    )
    units = w_down.shape[1]
    new_gate, new_up, new_down = (new[i * units : (i + 1) * units] for i in range(3))
    return (token_grad, new_gate.T[None], new_up.T[None], new_down[None])


def solution(mesh):
    return jax.shard_map(
        on_device,
        mesh=mesh,
        in_specs=(
            P("expert", "hidden"),
            P("expert", "hidden"),
            P("expert", None),
            P("expert", None),
            P(),
            P("expert", None, "hidden"),
            P("expert", None, "hidden"),
            P("expert", "hidden", None),
            P("expert", None, "hidden"),
            P("expert", None, "hidden"),
            P("expert", "hidden", None),
        ),
        out_specs=(
            P("expert", "hidden"),
            P("expert", None, "hidden"),
            P("expert", None, "hidden"),
            P("expert", "hidden", None),
        ),
        check_vma=False,
    )
```
